512 devices in a mesh: comp: 8 (over x, core), panel: 64 (over z, y).
Axes of the slice: x: 4, y: 4, z: 16, core: 2. Of those that a mesh axis runs over, the one named last changes fastest.
Arguments:
- state: float32 [8, 5, 64, 192, 256], P('comp', None, 'panel'), as said below
- time_step: float32 [8, 64, 192, 256], P('comp', 'panel'), may hold values from 10 to 40
- radius: float32 [8, 64, 192, 256], P('comp', 'panel'), may hold values from 0.5 to 4
- implicit_coeff: float32 [8, 3], P('comp'), may hold values from 9 to 36
- donor_cells: int32 [8, 64, 8, 512], P('comp', 'panel'), may hold values from 0 to 49151
- donor_weights: float32 [8, 64, 8, 512], P('comp', 'panel'), as said below
- donor_group: int32 [8, 64, 512, 1], P('comp', 'panel'), may hold values from 0 to 7; in each aligned block of 512 rows (0 to 511, 512 to 1023, ..., all dimensions but the last counted through in order) at most 128 rows name the same one
- recv_cells: int32 [8, 64, 8, 128], P('comp', 'panel'), may hold values from 0 to 49151, as said below
Outputs:
- delta: float32 [8, 5, 64, 192, 256], P('comp', None, 'panel')
The draws below stay inside these ranges and needn't reach their ends.
Inputs may be any that keep to these rules, and one draw needn't show every extreme that they name: `donor_weights`: the eight weights of a donor are positive and sum to one. `donor_group`: on one device no grid receives more than 128 donors, and some grid receives exactly 128 from some devices. `recv_cells`: the slab indices of one device are all distinct. `state`: density is positive.
All inputs are finite; a program needn't handle non-finite values.
Results may differ from the reference program's by a relative error of at most 0.0003.
Values sent between devices are 32-bit elements; how exact they have to be, the bound alone decides.
A program may use at most 128 MiB of HBM per device.

```python
import math
from functools import partial
import jax
import jax.numpy as jnp
import numpy as np
from jax import lax

NI = 256
NJ = 192
DON = 512
GRIDS = 8
NK = 64
CAP = 128
CELLS = 49152
N_COMP = 8
N_PANEL = 64


def draw_state(key, part):
    key_dens, key_vel, key_pres = jax.random.split(key, 3)
    shape_cells = (GRIDS, NK, NJ, NI)
    density = jax.random.uniform(key_dens, shape_cells, jnp.float32, 0.6, 1.6)
    velocity = jnp.clip(0.5 * jax.random.normal(key_vel, (3,) + shape_cells, jnp.float32), -1.5, 1.5)
    pressure = jax.random.uniform(key_pres, shape_cells, jnp.float32, 0.5, 1.5)
    momentum = density[None] * velocity
    energy = pressure / 0.4 + 0.5 * density * (velocity[0] * velocity[0] + velocity[1] * velocity[1] + velocity[2] * velocity[2])
    return jnp.concatenate([density[:, None], jnp.moveaxis(momentum, 0, 1), energy[:, None]], axis=1)


def draw_donor_weights(key, part):
    shape_all = (GRIDS, N_PANEL, 8, DON)
    raw = jax.random.uniform(key, shape_all, jnp.float32, 0.05, 1.0)
    return raw / jnp.sum(raw, axis=2, keepdims=True)


def draw_recv_cells(key, part):
    slots_all = N_COMP * CAP
    bucket = CELLS // slots_all
    key_off, key_perm = jax.random.split(jax.random.fold_in(key, 7))
    offsets = jax.random.randint(key_off, (GRIDS * N_PANEL, slots_all), 0, bucket)
    base_cells = jnp.arange(slots_all, dtype=jnp.int32)[None, :] * bucket + offsets
    perm_keys = jax.random.split(key_perm, GRIDS * N_PANEL)
    orders = jax.vmap(lambda one_key: jax.random.permutation(one_key, slots_all))(perm_keys)
    chosen = jnp.take_along_axis(base_cells, orders, axis=1)
    return chosen.reshape(GRIDS, N_PANEL, N_COMP, CAP).astype(jnp.int32)


def place_ends(array, key, least, high):
    longest = array.shape.index(max(array.shape))
    spots = []
    for shift in (0, 1):
        where = [jax.random.randint(jax.random.fold_in(key, axis), (), 0, length) for axis, length in enumerate(array.shape)]
        where[longest] = (where[longest] + shift) % array.shape[longest]
        spots.append(tuple(where))
    return array.at[spots[0]].set(least).at[spots[1]].set(high)


def steps_of(own_key, extent, cuts, smallest, largest):
    loudness = 1.0
    for axis_at, blocks in cuts:
        steps = jax.random.uniform(jax.random.fold_in(jax.random.fold_in(own_key, 6), axis_at), (blocks,), jnp.float32, smallest / len(cuts), largest / len(cuts))
        loudness = loudness * jnp.repeat(jnp.exp(steps), extent[axis_at] // blocks).reshape((-1,) + (1,) * (len(extent) - 1 - axis_at))
    return loudness


def deal_out(stream_key, own, number, rows, number_of, top, most, slope):
    sequence = jax.random.permutation(stream_key, number_of)
    heavy_load, usual = portions_of(number_of, rows * top, most, slope, True), portions_of(number_of, rows * top, most, slope, False)
    places = jnp.arange(number_of)

    def named(lengths, offset_by):
        used = int((lengths > 0).sum())
        fixed = max(1, used // 4)
        passed = fixed + (places - fixed + offset_by * (used - fixed)) % max(1, number_of - fixed)
        return jnp.zeros((number_of,), jnp.int32).at[sequence[jnp.where(places < fixed, places, passed)]].set(jnp.asarray(lengths, jnp.int32))

    lengths = jnp.where(number % 4 == 0, named(heavy_load, number // 4), named(usual, number - number // 4 - 1))
    mixed = jax.random.permutation(jax.random.fold_in(own, 3), number_of)
    giver, receiver = mixed[0:number_of // 2 * 2:2], mixed[1:number_of // 2 * 2:2]
    margin = jnp.minimum(lengths[giver] - 1, most - lengths[receiver]) // 2
    margin = jnp.where((giver == sequence[0]) | (receiver == sequence[0]) | (lengths[receiver] == 0), 0, jnp.maximum(margin, 0))
    passed = jax.random.randint(jax.random.fold_in(own, 4), (number_of // 2,), 0, 1 << 20) % (margin + 1)
    lengths = lengths.at[giver].add(-passed).at[receiver].add(passed)
    members = jnp.searchsorted(jnp.cumsum(lengths), jnp.arange(rows * top), side="right").astype(jnp.int32)
    listing = members.reshape(top, rows).T
    listing = listing[jax.random.permutation(jax.random.fold_in(own, 1), rows)]
    offset_by = jax.random.randint(jax.random.fold_in(own, 2), (rows, 1), 0, top)
    return jnp.take_along_axis(listing, (jnp.arange(top)[None, :] + offset_by) % top, axis=1)


def portions_of(number_of, total, bound, skew, full):
    loads = [(1 << 20) // math.isqrt(standing ** skew) + 1 for standing in range(1, number_of + 1)]
    largest = bound if full else min(bound, max(-(-total // number_of), total * loads[0] // sum(loads)))
    least = 1 if total - largest >= number_of - 1 else 0
    holding, spare = [largest] + [least] * (number_of - 1), total - largest - least * (number_of - 1)
    while spare > 0:
        free = [i for i in range(1, number_of) if holding[i] < largest] or [i for i in range(1, number_of) if holding[i] < bound]
        mass, budget = sum([loads[i] for i in free]), spare
        for i in free:
            more = min(bound - holding[i], max(1, budget * loads[i] // mass), spare)
            holding[i] = holding[i] + more
            spare = spare - more
    return np.array(holding)


def setup_inputs(seed: int = 0) -> dict:
    streams_of = jax.random.split(jax.random.key(seed), 9)
    state = draw_state(jax.random.fold_in(streams_of[8], 71), 0)
    time_step = jnp.clip(jnp.exp(math.log(40.0) - 1.3862944 * jax.random.uniform(streams_of[1], (GRIDS, NK, NJ, NI), jnp.float32) ** steps_of(streams_of[1], (GRIDS, NK, NJ, NI), ((0, 8), (1, 64)), -0.2, 0.2)), 10.0, 40.0)
    radius = jnp.clip(jnp.exp(math.log(4.0) - 2.0794415 * jax.random.uniform(streams_of[2], (GRIDS, NK, NJ, NI), jnp.float32) ** steps_of(streams_of[2], (GRIDS, NK, NJ, NI), ((0, 8), (1, 64)), -0.2, 0.2)), 0.5, 4.0)
    implicit_coeff = jnp.clip(jnp.exp(math.log(36.0) - 1.3862944 * jax.random.uniform(streams_of[3], (GRIDS, 3), jnp.float32) ** steps_of(streams_of[3], (GRIDS, 3), ((0, 8),), -0.2, 0.2)), 9.0, 36.0)
    donor_cells = place_ends(jax.random.randint(streams_of[4], (GRIDS, N_PANEL, 8, DON), 0, CELLS), jax.random.fold_in(streams_of[4], 1), 0, CELLS - 1).astype(jnp.int32)
    donor_weights = draw_donor_weights(jax.random.fold_in(streams_of[8], 71), 0)
    donor_group_keys = jax.random.split(jax.random.fold_in(streams_of[6], 1), GRIDS * N_PANEL * DON // DON)
    donor_group_turns = jax.random.permutation(jax.random.fold_in(streams_of[6], 3), GRIDS * N_PANEL * DON // DON)
    donor_group = jax.vmap(lambda own, number: deal_out(jax.random.fold_in(streams_of[6], 2), own, number, DON, N_COMP, 1, CAP, 2))(donor_group_keys, donor_group_turns).reshape((GRIDS, N_PANEL, DON, 1))
    recv_cells = draw_recv_cells(jax.random.fold_in(streams_of[8], 71), 0)
    return dict(state=state, time_step=time_step, radius=radius, implicit_coeff=implicit_coeff, donor_cells=donor_cells, donor_weights=donor_weights, donor_group=donor_group, recv_cells=recv_cells)


GAS_FACTOR = 0.4
EXPLICIT_FOURTH = 0.0625
IMPLICIT_SECOND = 1.0
IMPLICIT_FOURTH = 0.125

def direction_flux(field, direction, density):
    speed = field[direction] / density
    pressure = GAS_FACTOR * (field[4] - 0.5 * (field[1] * field[1] + field[2] * field[2] + field[3] * field[3]) / density)
    rows_out = [field[direction]]
    for member in (1, 2, 3):
        if member == direction:
            rows_out.append(field[member] * speed + pressure)
        else:
            rows_out.append(field[member] * speed)
    rows_out.append((field[4] + pressure) * speed)
    return jnp.stack(rows_out)

def central(values, axis):
    length = values.shape[axis]
    widths = [(0, 0)] * values.ndim
    widths[axis] = (1, 1)
    padded = jnp.pad(values, widths)
    return 0.5 * (lax.slice_in_dim(padded, 2, length + 2, axis=axis) - lax.slice_in_dim(padded, 0, length, axis=axis))

def fourth(values, axis):
    length = values.shape[axis]
    widths = [(0, 0)] * values.ndim
    widths[axis] = (2, 2)
    padded = jnp.pad(values, widths)
    parts = [lax.slice_in_dim(padded, shift_by, shift_by + length, axis=axis) for shift_by in range(5)]
    return parts[0] - 4.0 * parts[1] + 6.0 * parts[2] - 4.0 * parts[3] + parts[4]

def line_inverse(length, coeff):
    index = jnp.arange(length)
    gap = jnp.abs(index[:, None] - index[None, :])
    matrix = jnp.where(gap == 0, 1.0 + coeff * (2.0 * IMPLICIT_SECOND + 6.0 * IMPLICIT_FOURTH), jnp.where(gap == 1, -coeff * (IMPLICIT_SECOND + 4.0 * IMPLICIT_FOURTH), jnp.where(gap == 2, coeff * IMPLICIT_FOURTH, 0.0 * coeff)))
    factor = jnp.linalg.cholesky(matrix)
    identity = jnp.eye(length, dtype=matrix.dtype)
    lower_part = lax.linalg.triangular_solve(factor, identity, left_side=True, lower=True)
    return lax.linalg.triangular_solve(factor, lower_part, left_side=True, lower=True, transpose_a=True)

def interpolate(grid_slab, cells, weights):
    return jnp.sum(grid_slab[:, cells] * weights[None], axis=1)

def pack_slots(donor_values, group_col, count, capacity):
    onehot = (group_col[:, None] == jnp.arange(count, dtype=jnp.int32)[None, :]).astype(jnp.int32)
    ranks = jnp.sum((jnp.cumsum(onehot, axis=0) - 1) * onehot, axis=1).astype(jnp.int32)
    target = (group_col * capacity + ranks).astype(jnp.int32)
    buffer = jnp.zeros((5, count * capacity), donor_values.dtype).at[:, target].set(donor_values)
    live = jnp.zeros((count * capacity,), donor_values.dtype).at[target].set(1.0)
    return (buffer.reshape(5, count, capacity).transpose(1, 0, 2), live.reshape(count, 1, capacity))

def place_fringe(grid_slab, got_values, got_live, targets):
    flat_values = got_values.transpose(1, 0, 2).reshape(5, -1)
    flat_live = got_live.reshape(-1)
    flat_cells = targets.reshape(-1)
    current = grid_slab[:, flat_cells]
    return grid_slab.at[:, flat_cells].set(jnp.where(flat_live[None, :] > 0.5, flat_values, current))

def grid_delta(packed):
    field, step_size, spread, coeffs = packed
    density = field[0]
    convect = central(direction_flux(field, 1, density), 3) + central(direction_flux(field, 2, density), 2) + central(direction_flux(field, 3, density), 1)
    smooth = fourth(field, 3) + fourth(field, 2) + fourth(field, 1)
    rhs = step_size * (-convect - EXPLICIT_FOURTH * spread * smooth)
    inverse_k = line_inverse(NK, coeffs[2])
    inverse_j = line_inverse(NJ, coeffs[1])
    inverse_i = line_inverse(NI, coeffs[0])
    result = jnp.einsum('ab,vbji->vaji', inverse_k, rhs, precision=lax.Precision.HIGHEST)
    result = jnp.einsum('ab,vkbi->vkai', inverse_j, result, precision=lax.Precision.HIGHEST)
    result = jnp.einsum('ab,vkjb->vkja', inverse_i, result, precision=lax.Precision.HIGHEST)
    return result

def reference(state, time_step, radius, implicit_coeff, donor_cells, donor_weights, donor_group, recv_cells):
    devices_all = GRIDS * N_PANEL
    slabs = state.reshape(GRIDS, 5, N_PANEL, CELLS).transpose(0, 2, 1, 3).reshape(devices_all, 5, CELLS)
    cells = donor_cells.reshape(devices_all, 8, DON)
    weights = donor_weights.reshape(devices_all, 8, DON)
    groups = donor_group.reshape(devices_all, DON)
    donor_values = jax.vmap(interpolate)(slabs, cells, weights)
    buffers, lives = jax.vmap(partial(pack_slots, count=N_COMP, capacity=CAP))(donor_values, groups)
    got_values = buffers.reshape(GRIDS, N_PANEL, N_COMP, 5, CAP).transpose(2, 1, 0, 3, 4).reshape(devices_all, N_COMP, 5, CAP)
    got_live = lives.reshape(GRIDS, N_PANEL, N_COMP, 1, CAP).transpose(2, 1, 0, 3, 4).reshape(devices_all, N_COMP, 1, CAP)
    targets = recv_cells.reshape(devices_all, N_COMP, CAP)
    fringed = jax.vmap(place_fringe)(slabs, got_values, got_live, targets)
    fringe_state = fringed.reshape(GRIDS, N_PANEL, 5, CELLS).transpose(0, 2, 1, 3).reshape(GRIDS, 5, NK, NJ, NI)
    return lax.map(grid_delta, (fringe_state, time_step, radius, implicit_coeff))
```

```python
import functools

import jax
import jax.numpy as jnp
from jax import lax
from jax.experimental import pallas as pl
from jax.experimental.pallas import tpu as pltpu
from jax.sharding import PartitionSpec as P

MESH = pl.DeviceIdType.MESH
F32, BF16 = jnp.float32, jnp.bfloat16
NV = 5
NY = 4
PAD = 8
ROWS = 16


def parts(x):
    hi = x.astype(BF16)
    rest = x - hi.astype(F32)
    mid = rest.astype(BF16)
    return hi, mid, (rest - mid.astype(F32)).astype(BF16)


def inverse_entries(h, length, i, j):
    root = jnp.sqrt(16.0 - 8.0 / h)
    m1, m2 = (8.0 / h) / (4.0 + root), 4.0 + root
    n = float(length)

    def green(m, a, b):
        s = 0.5 * jnp.sqrt(m)
        t = 2.0 * jnp.log(s + jnp.sqrt(1.0 + s * s))
        d = jnp.abs(a - b)
        top = (
            jnp.exp(-t * d)
            - jnp.exp(-t * (a + b + 2.0))
            - jnp.exp(-t * (2.0 * n - a - b))
            + jnp.exp(-t * (2.0 * n + 2.0 - d))
        )
        two_sinh = jnp.exp(t) - jnp.exp(-t)
        return top / (two_sinh * (1.0 - jnp.exp(-2.0 * t * (n + 1.0))))

    def smooth(a, b):
        return (8.0 / h) * (green(m1, a, b) - green(m2, a, b)) / (m2 - m1)

    zero = jnp.zeros_like(h)
    corner, across = smooth(zero, zero), smooth(zero, zero + (n - 1.0))
    even_scale = 0.5 / (8.0 / h + corner + across)
    odd_scale = 0.5 / (8.0 / h + corner - across)
    i0, i1 = smooth(i, zero), smooth(i, zero + (n - 1.0))
    j0, j1 = smooth(j, zero), smooth(j, zero + (n - 1.0))
    return (
        smooth(i, j)
        - even_scale * (i0 + i1) * (j0 + j1)
        - odd_scale * (i0 - i1) * (j0 - j1)
    )


def iota(shape, axis):
    return lax.broadcasted_iota(jnp.int32, shape, axis)


def donor_kernel(state, cells, weights, group, packed, left, acc):
    nv, nj, ni = state.shape
    n_c, don = cells.shape
    count = packed.shape[1] // 128
    width = min(256, don)
    flat = state[...].reshape(nv * nj, ni)
    for k, part in enumerate(parts(flat)):
        left[:, k * ni : (k + 1) * ni] = part
    acc[...] = jnp.zeros_like(acc)

    for block in range(don // width):
        span = slice(block * width, (block + 1) * width)

        def one(c, carry):
            cell = cells[pl.ds(c, 1), span]
            weight = weights[pl.ds(c, 1), span]
            col = jnp.where(iota((ni, width), 0) == cell % ni, 1.0, 0.0).astype(BF16)
            got = jnp.dot(
                left[...], jnp.concatenate([col, col, col], axis=0), preferred_element_type=F32
            )
            row = jnp.where(iota((nj, width), 0) == cell // ni, weight, 0.0)
            for v in range(nv):
                term = got[v * nj : (v + 1) * nj] * row
                acc[v, :, span] += jnp.sum(term.reshape(nj // 8, 8, width), axis=0)
            return carry

        lax.fori_loop(0, n_c, one, 0)

    values = [jnp.sum(acc[v], axis=0, keepdims=True) for v in range(nv)]
    values = jnp.concatenate(
        values + [jnp.ones((1, don), F32), jnp.zeros((8 - nv - 1, don), F32)], axis=0
    )
    mine = group[...]
    hot = jnp.where(iota((don, 128), 1) == mine, 1.0, 0.0)
    before = jnp.where(iota((don, don), 1) < iota((don, don), 0), 1.0, 0.0).astype(BF16)
    ahead = jnp.dot(before, hot.astype(BF16), preferred_element_type=F32)
    slot = jnp.sum(hot * ahead, axis=1, keepdims=True).astype(jnp.int32)
    target = mine * 128 + slot
    place = jnp.where(iota((don, count * 128), 1) == target, 1.0, 0.0).astype(BF16)
    hi, mid, lo = parts(values)
    packed[...] = (
        jnp.dot(hi, place, preferred_element_type=F32)
        + jnp.dot(mid, place, preferred_element_type=F32)
        + jnp.dot(lo, place, preferred_element_type=F32)
    )


def flux(f, direction):
    rho = jnp.where(f[0] > 0.0, f[0], 1.0)
    inv = 1.0 / rho
    speed = f[direction] * inv
    pressure = 0.4 * (f[4] - 0.5 * (f[1] * f[1] + f[2] * f[2] + f[3] * f[3]) * inv)
    out = [f[direction]]
    for member in (1, 2, 3):
        term = f[member] * speed
        out.append(term + pressure if member == direction else term)
    out.append((f[4] + pressure) * speed)
    return out


def step_kernel(
    nc, nz, state, step_size, radius, coeff, packed, cells, out,
    got, vals, full, slab, local, own, lin, lout, rin, rout, done, back, inv_j, inv_i, lhs, coef,
    fx_send, fx_recv, tr_send, tr_recv, ya_send, ya_recv, zh_send, zh_recv, sc_send, sc_recv, yb_send, yb_recv,
):
    _, nj, ni = state.shape
    quarter = nj // NY
    tall = quarter + 2 * PAD
    blocks = quarter // ROWS
    chunks = blocks * NV
    slots = vals.shape[1]
    me = lax.axis_index("comp")
    panel = lax.axis_index("panel")
    z, y = panel // NY, panel % NY
    low, high = (z + nz - 1) % nz, (z + 1) % nz

    def at(comp, z_, y_):
        return (comp, z_ * NY + y_)

    barrier = pltpu.get_barrier_semaphore()
    for d in range(1, nc):
        pl.semaphore_signal(barrier, inc=1, device_id=at((me + d) % nc, z, y), device_id_type=MESH)
    for d in range(1, NY):
        pl.semaphore_signal(barrier, inc=1, device_id=at(me, z, (y + d) % NY), device_id_type=MESH)
    pl.semaphore_signal(barrier, inc=1, device_id=at(me, low, y), device_id_type=MESH)
    pl.semaphore_signal(barrier, inc=1, device_id=at(me, high, y), device_id_type=MESH)
    pl.semaphore_wait(barrier, nc - 1 + NY - 1 + 2)

    def fringe(d):
        peer = (me + d) % nc
        return pltpu.make_async_remote_copy(
            src_ref=packed.at[:, pl.ds(pl.multiple_of(peer * 128, 128), 128)],
            dst_ref=got.at[me],
            send_sem=fx_send.at[d],
            recv_sem=fx_recv.at[d],
            device_id=at(peer, z, y),
            device_id_type=MESH,
        )

    for d in range(1, nc):
        fringe(d).start()

    def local_copy(which, d):
        to = (y + d) % NY
        return pltpu.make_async_remote_copy(
            src_ref=(step_size, radius)[which].at[pl.ds(pl.multiple_of(to * quarter, 8), quarter), :],
            dst_ref=local.at[which, y],
            send_sem=tr_send.at[which, d],
            recv_sem=tr_recv.at[which, d],
            device_id=at(me, z, to),
            device_id_type=MESH,
        )

    for which in range(2):
        for d in range(1, NY):
            local_copy(which, d).start()
    mine = pl.ds(pl.multiple_of(y * quarter, 8), quarter)
    local[0, y] = step_size[mine, :]
    local[1, y] = radius[mine, :]

    h2 = jnp.full((8, 128), coeff[0, 2], F32)
    base = (z * NY - 2).astype(F32)
    k_near = inverse_entries(
        h2,
        nz * NY,
        jnp.maximum(iota((8, 128), 0).astype(F32) + base, 0.0),
        jnp.maximum(iota((8, 128), 1).astype(F32) + base, 0.0),
    )

    def entry(a, b):
        return k_near[a : a + 1, b : b + 1]

    for q in range(4):
        for l in range(4):
            coef[q * 4 + l] = entry(2 + q, 2 + l)[0, 0]
    for side, first in ((0, 0), (1, 6)):
        a, b, d = entry(first, first), entry(first, first + 1), entry(first + 1, first + 1)
        det = 1.0 / (a * d - b * b)
        edge = (z == 0) if side == 0 else (z == nz - 1)
        for q in range(4):
            s, t = entry(2 + q, first), entry(2 + q, first + 1)
            coef[16 + side * 8 + q * 2] = jnp.where(edge, 0.0, ((s * d - t * b) * det)[0, 0])
            coef[16 + side * 8 + q * 2 + 1] = jnp.where(edge, 0.0, ((t * a - s * b) * det)[0, 0])

    for ref, length, which in ((inv_j, nj, 1), (inv_i, ni, 0)):
        ref[...] = inverse_entries(
            jnp.full((1, 1), coeff[0, which], F32),
            length,
            iota((length, 1), 0).astype(F32),
            iota((1, length), 1).astype(F32),
        )

    got[me] = packed[:, pl.ds(pl.multiple_of(me * 128, 128), 128)]
    for d in range(1, nc):
        fringe(d).wait_recv()
    for g in range(nc):
        vals[:, g * 128 : (g + 1) * 128] = got[g]
    cell = jnp.concatenate([cells[g : g + 1, :] for g in range(nc)], axis=1)
    hot_i = jnp.where(iota((ni, slots), 0) == cell % ni, 1.0, 0.0).astype(BF16)
    hit = iota((nj, slots), 0) == cell // ni
    dims = (((1,), (1,)), ((), ()))
    live = jnp.where(hit, vals[NV : NV + 1, :], 0.0).astype(BF16)
    filled = lax.dot_general(live, hot_i, dims, preferred_element_type=F32) > 0.5
    for v in range(NV):
        for k, part in enumerate(parts(vals[v : v + 1, :])):
            lhs[k * nj : (k + 1) * nj, :] = jnp.where(hit, part.astype(F32), 0.0).astype(BF16)
        put = lax.dot_general(lhs[...], hot_i, dims, preferred_element_type=F32)
        put = put[:nj] + put[nj : 2 * nj] + put[2 * nj :]
        full[v, :PAD] = jnp.zeros((PAD, ni), F32)
        full[v, PAD + nj :] = jnp.zeros((PAD, ni), F32)
        full[v, PAD : PAD + nj] = jnp.where(filled, put, state[v])

    def quarter_copy(v, d):
        to = (y + d) % NY
        return pltpu.make_async_remote_copy(
            src_ref=full.at[v, pl.ds(pl.multiple_of(to * quarter, 8), tall), :],
            dst_ref=slab.at[2 + y, v],
            send_sem=ya_send.at[v, d],
            recv_sem=ya_recv.at[v, d],
            device_id=at(me, z, to),
            device_id_type=MESH,
        )

    def halo_copy(v, side):
        return pltpu.make_async_remote_copy(
            src_ref=slab.at[pl.ds(4 - 2 * side, 2), v, pl.ds(PAD, quarter), :],
            dst_ref=slab.at[pl.ds(6 * side, 2), v, pl.ds(PAD, quarter), :],
            send_sem=zh_send.at[v, side],
            recv_sem=zh_recv.at[v, side],
            device_id=at(me, (high, low)[side], y),
            device_id_type=MESH,
        )

    for v in range(NV):
        for d in range(1, NY):
            quarter_copy(v, d).start()
    for v in range(NV):
        slab[2 + y, v] = full[v, pl.ds(pl.multiple_of(y * quarter, 8), tall), :]

    @pl.when(z == 0)
    def _():
        slab[0:2] = jnp.zeros((2, NV, tall, ni), F32)

    @pl.when(z == nz - 1)
    def _():
        slab[6:8] = jnp.zeros((2, NV, tall, ni), F32)

    for v in range(NV):
        for d in range(1, NY):
            quarter_copy(v, d).wait_recv()

        @pl.when(z < nz - 1)
        def _():
            halo_copy(v, 0).start()

        @pl.when(z > 0)
        def _():
            halo_copy(v, 1).start()

    for which in range(2):
        for d in range(1, NY):
            local_copy(which, d).wait_recv()
    for v in range(NV):

        @pl.when(z > 0)
        def _():
            halo_copy(v, 0).wait_recv()

        @pl.when(z < nz - 1)
        def _():
            halo_copy(v, 1).wait_recv()

    lane = iota((ROWS, ni), 1)
    for rb in range(blocks):
        top = PAD + rb * ROWS

        def layer(l, carry):
            def load(dl, dj):
                return [slab[2 + l + dl, v, top + dj : top + dj + ROWS, :] for v in range(NV)]

            here = load(0, 0)

            def shifted(by):
                keep = (lane + by >= 0) & (lane + by < ni)
                return [jnp.where(keep, pltpu.roll(f, (-by) % ni, 1), 0.0) for f in here]

            convect, near, far = None, None, None
            for direction, look in (
                (1, shifted),
                (2, lambda by: load(0, by)),
                (3, lambda by: load(by, 0)),
            ):
                ahead, behind = look(1), look(-1)
                diff = [a - b for a, b in zip(flux(ahead, direction), flux(behind, direction))]
                one = [a + b for a, b in zip(ahead, behind)]
                two = [a + b for a, b in zip(look(2), look(-2))]
                convect = diff if convect is None else [a + b for a, b in zip(convect, diff)]
                near = one if near is None else [a + b for a, b in zip(near, one)]
                far = two if far is None else [a + b for a, b in zip(far, two)]
            dt = local[0, l, rb * ROWS : (rb + 1) * ROWS, :]
            spread = 0.0625 * local[1, l, rb * ROWS : (rb + 1) * ROWS, :]
            for v in range(NV):
                smooth = far[v] - 4.0 * near[v] + 18.0 * here[v]
                done[l, rb * NV + v] = dt * (-0.5 * convect[v] - spread * smooth)
            return carry

        lax.fori_loop(0, NY, layer, 0)

        def block(v, carry):
            t = rb * NV + v
            rhs = [done[l, t] for l in range(NY)]
            for q in range(NY):
                own[q, t] = (
                    coef[q * 4] * rhs[0]
                    + coef[q * 4 + 1] * rhs[1]
                    + coef[q * 4 + 2] * rhs[2]
                    + coef[q * 4 + 3] * rhs[3]
                )
            return carry

        lax.fori_loop(0, NV, block, 0)

    @pl.when(z == 0)
    def _():
        lin[...] = jnp.zeros_like(lin)

    @pl.when(z == nz - 1)
    def _():
        rin[...] = jnp.zeros_like(rin)

    def pass_on(t, side):
        return pltpu.make_async_remote_copy(
            src_ref=(lout, rout)[side].at[t],
            dst_ref=(lin, rin)[side].at[t],
            send_sem=sc_send.at[side, t],
            recv_sem=sc_recv.at[side, t],
            device_id=at(me, (high, low)[side], y),
            device_id_type=MESH,
        )

    def home(t, q):
        return pltpu.make_async_remote_copy(
            src_ref=done.at[q, t],
            dst_ref=back.at[t % NV, pl.ds(pl.multiple_of(y * quarter + t // NV * ROWS, ROWS), ROWS), :],
            send_sem=yb_send.at[t, q],
            recv_sem=yb_recv.at[t, y],
            device_id=at(me, z, q),
            device_id_type=MESH,
        )

    def home_from(t, s):
        return pltpu.make_async_remote_copy(
            src_ref=done.at[s, t],
            dst_ref=back.at[t % NV, pl.ds(pl.multiple_of(s * quarter + t // NV * ROWS, ROWS), ROWS), :],
            send_sem=yb_send.at[t, s],
            recv_sem=yb_recv.at[t, s],
            device_id=at(me, z, s),
            device_id_type=MESH,
        )

    def scan_step(t, side):
        starts, ends = (z > 0, z < nz - 1) if side == 0 else (z < nz - 1, z > 0)
        came, gone = ((lin, lout), (rin, rout))[side]

        @pl.when(starts)
        def _():
            pass_on(t, side).wait_recv()

        @pl.when(ends)
        def _():
            first, second = came[t, 0], came[t, 1]
            for m in range(2):
                q = 2 + m if side == 0 else m
                at_q = 16 + side * 8 + q * 2
                gone[t, m] = own[q, t] + coef[at_q] * first + coef[at_q + 1] * second
            pass_on(t, side).start()

    def finish(t):
        l0, l1, r0, r1 = lin[t, 0], lin[t, 1], rin[t, 0], rin[t, 1]
        for q in range(NY):
            total = (
                own[q, t]
                + (coef[16 + q * 2] * l0 + coef[17 + q * 2] * l1)
                + (coef[24 + q * 2] * r0 + coef[25 + q * 2] * r1)
            )
            done[q, t] = total

            @pl.when(y == q)
            def _():
                back[t % NV, pl.ds(pl.multiple_of(y * quarter + t // NV * ROWS, ROWS), ROWS), :] = total

            @pl.when(y != q)
            def _():
                home(t, q).start()

    lag = jnp.clip(3 * (nz - 1 - 2 * z), -chunks, chunks)
    l_from, r_from = jnp.maximum(-lag, 0), jnp.maximum(lag, 0)
    last = jnp.maximum(l_from, r_from)

    def tick(s, carry):
        for t, job in (
            (s - l_from, lambda t: scan_step(t, 0)),
            (s - r_from, lambda t: scan_step(t, 1)),
            (s - last, finish),
        ):

            @pl.when((t >= 0) & (t < chunks))
            def _():
                job(t)

        return carry

    lax.fori_loop(0, 2 * chunks, tick, 0)

    def solve(v, carry):
        for rb in range(blocks):
            for s in range(NY):

                @pl.when(y != s)
                def _():
                    home_from(rb * NV + v, s).wait_recv()

        half = jnp.dot(
            inv_j[...], back[v], preferred_element_type=F32, precision=lax.Precision.HIGHEST
        )
        out[v] = jnp.dot(
            half, inv_i[...], preferred_element_type=F32, precision=lax.Precision.HIGHEST
        )
        return carry

    lax.fori_loop(0, NV, solve, 0)

    for d in range(1, nc):
        fringe(d).wait_send()
    for d in range(1, NY):
        for which in range(2):
            local_copy(which, d).wait_send()
        for v in range(NV):
            quarter_copy(v, d).wait_send()
    for v in range(NV):

        @pl.when(z < nz - 1)
        def _():
            halo_copy(v, 0).wait_send()

        @pl.when(z > 0)
        def _():
            halo_copy(v, 1).wait_send()

    def drain(t, carry):
        @pl.when(z < nz - 1)
        def _():
            pass_on(t, 0).wait_send()

        @pl.when(z > 0)
        def _():
            pass_on(t, 1).wait_send()

        for q in range(NY):

            @pl.when(y != q)
            def _():
                home(t, q).wait_send()

        return carry

    lax.fori_loop(0, chunks, drain, 0)


def vmem():
    return pl.BlockSpec(memory_space=pltpu.VMEM)


def body(nc, nz, state, time_step, radius, coeff, donor_cells, donor_weights, donor_group, recv_cells):
    _, nv, _, nj, ni = state.shape
    slots = recv_cells.shape[2] * recv_cells.shape[3]
    don = donor_cells.shape[3]
    quarter = nj // NY
    chunks = quarter // ROWS * NV
    field = state.reshape(nv, nj, ni)
    packed = pl.pallas_call(
        donor_kernel,
        out_shape=jax.ShapeDtypeStruct((8, slots), F32),
        in_specs=[vmem()] * 4,
        out_specs=vmem(),
        scratch_shapes=[pltpu.VMEM((nv * nj, 3 * ni), BF16), pltpu.VMEM((nv, 8, don), F32)],
        compiler_params=pltpu.CompilerParams(vmem_limit_bytes=40 * 2**20),
        name="donors",
    )(
        field,
        donor_cells.reshape(donor_cells.shape[2:]),
        donor_weights.reshape(donor_weights.shape[2:]),
        donor_group.reshape(don, 1),
    )
    dma = pltpu.SemaphoreType.DMA
    delta = pl.pallas_call(
        functools.partial(step_kernel, nc, nz),
        out_shape=jax.ShapeDtypeStruct((nv, nj, ni), F32),
        in_specs=[vmem()] * 3 + [pl.BlockSpec(memory_space=pltpu.SMEM)] + [vmem()] * 2,
        out_specs=vmem(),
        scratch_shapes=[
            pltpu.VMEM((nc, 8, 128), F32),
            pltpu.VMEM((8, slots), F32),
            pltpu.VMEM((nv, nj + 2 * PAD, ni), F32),
            pltpu.VMEM((2 * NY, nv, quarter + 2 * PAD, ni), F32),
            pltpu.VMEM((2, NY, quarter, ni), F32),
            pltpu.VMEM((NY, chunks, ROWS, ni), F32),
            pltpu.VMEM((chunks, 2, ROWS, ni), F32),
            pltpu.VMEM((chunks, 2, ROWS, ni), F32),
            pltpu.VMEM((chunks, 2, ROWS, ni), F32),
            pltpu.VMEM((chunks, 2, ROWS, ni), F32),
            pltpu.VMEM((NY, chunks, ROWS, ni), F32),
            pltpu.VMEM((nv, nj, ni), F32),
            pltpu.VMEM((nj, nj), F32),
            pltpu.VMEM((ni, ni), F32),
            pltpu.VMEM((3 * nj, slots), BF16),
            pltpu.SMEM((32,), F32),
            dma((nc,)), dma((nc,)),
            dma((2, NY)), dma((2, NY)),
            dma((nv, NY)), dma((nv, NY)),
            dma((nv, 2)), dma((nv, 2)),
            dma((2, chunks)), dma((2, chunks)),
            dma((chunks, NY)), dma((chunks, NY)),
        ],
        compiler_params=pltpu.CompilerParams(
            collective_id=0, has_side_effects=True, vmem_limit_bytes=48 * 2**20
        ),
        name="step",
    )(
        field,
        time_step.reshape(nj, ni),
        radius.reshape(nj, ni),
        coeff,
        packed,
        recv_cells.reshape(recv_cells.shape[2:]),
    )
    return delta.reshape(state.shape)


def solution(mesh):
    slabs = P("comp", "panel", None, None)
    whole = P("comp", None, "panel", None, None)
    return jax.shard_map(
        functools.partial(body, mesh.shape["comp"], mesh.shape["panel"] // NY),
        mesh=mesh,
        in_specs=(whole, slabs, slabs, P("comp", None), slabs, slabs, slabs, slabs),
        out_specs=whole,
        check_vma=False,
    )
```

```python
import functools

import jax
import jax.numpy as jnp
from jax import lax
from jax.experimental import pallas as pl
from jax.experimental.pallas import tpu as pltpu
from jax.sharding import PartitionSpec as P

MESH = pl.DeviceIdType.MESH
F32, BF16 = jnp.float32, jnp.bfloat16
NV = 5
NY = 4
PAD = 8
LAG = 6
ROWS = 16


def parts(x):
    hi = x.astype(BF16)
    rest = x - hi.astype(F32)
    mid = rest.astype(BF16)
    return hi, mid, (rest - mid.astype(F32)).astype(BF16)


def inverse_entries(h, length, i, j):
    root = jnp.sqrt(16.0 - 8.0 / h)
    m1, m2 = (8.0 / h) / (4.0 + root), 4.0 + root
    n = float(length)

    def green(m, a, b):
        s = 0.5 * jnp.sqrt(m)
        t = 2.0 * jnp.log(s + jnp.sqrt(1.0 + s * s))
        d = jnp.abs(a - b)
        top = (
            jnp.exp(-t * d)
            - jnp.exp(-t * (a + b + 2.0))
            - jnp.exp(-t * (2.0 * n - a - b))
            + jnp.exp(-t * (2.0 * n + 2.0 - d))
        )
        two_sinh = jnp.exp(t) - jnp.exp(-t)
        return top / (two_sinh * (1.0 - jnp.exp(-2.0 * t * (n + 1.0))))

    def smooth(a, b):
        return (8.0 / h) * (green(m1, a, b) - green(m2, a, b)) / (m2 - m1)

    zero = jnp.zeros_like(h)
    corner, across = smooth(zero, zero), smooth(zero, zero + (n - 1.0))
    even_scale = 0.5 / (8.0 / h + corner + across)
    odd_scale = 0.5 / (8.0 / h + corner - across)
    i0, i1 = smooth(i, zero), smooth(i, zero + (n - 1.0))
    j0, j1 = smooth(j, zero), smooth(j, zero + (n - 1.0))
    return (
        smooth(i, j)
        - even_scale * (i0 + i1) * (j0 + j1)
        - odd_scale * (i0 - i1) * (j0 - j1)
    )


def iota(shape, axis):
    return lax.broadcasted_iota(jnp.int32, shape, axis)


def donors(state, cells, weights, group, packed, left, acc):
    nv, nj, ni = state.shape
    n_c, don = cells.shape
    count = packed.shape[1] // 128
    width = min(256, don)
    flat = state[...].reshape(nv * nj, ni)
    for k, part in enumerate(parts(flat)):
        left[:, k * ni : (k + 1) * ni] = part
    acc[...] = jnp.zeros_like(acc)

    for block in range(don // width):
        span = slice(block * width, (block + 1) * width)

        def one(c, carry):
            cell = cells[pl.ds(c, 1), span]
            weight = weights[pl.ds(c, 1), span]
            col = jnp.where(iota((ni, width), 0) == cell % ni, 1.0, 0.0).astype(BF16)
            got = jnp.dot(
                left[...], jnp.concatenate([col, col, col], axis=0), preferred_element_type=F32
            )
            row = jnp.where(iota((nj, width), 0) == cell // ni, weight, 0.0)
            for v in range(nv):
                term = got[v * nj : (v + 1) * nj] * row
                acc[v, :, span] += jnp.sum(term.reshape(nj // 8, 8, width), axis=0)
            return carry

        lax.fori_loop(0, n_c, one, 0)

    values = [jnp.sum(acc[v], axis=0, keepdims=True) for v in range(nv)]
    values = jnp.concatenate(
        values + [jnp.ones((1, don), F32), jnp.zeros((8 - nv - 1, don), F32)], axis=0
    )
    mine = group[...]
    hot = jnp.where(iota((don, 128), 1) == mine, 1.0, 0.0)
    before = jnp.where(iota((don, don), 1) < iota((don, don), 0), 1.0, 0.0).astype(BF16)
    ahead = jnp.dot(before, hot.astype(BF16), preferred_element_type=F32)
    slot = jnp.sum(hot * ahead, axis=1, keepdims=True).astype(jnp.int32)
    target = mine * 128 + slot
    place = jnp.where(iota((don, count * 128), 1) == target, 1.0, 0.0).astype(BF16)
    hi, mid, lo = parts(values)
    packed[...] = (
        jnp.dot(hi, place, preferred_element_type=F32)
        + jnp.dot(mid, place, preferred_element_type=F32)
        + jnp.dot(lo, place, preferred_element_type=F32)
    )


def flux(f, direction):
    rho = jnp.where(f[0] > 0.0, f[0], 1.0)
    inv = 1.0 / rho
    speed = f[direction] * inv
    pressure = 0.4 * (f[4] - 0.5 * (f[1] * f[1] + f[2] * f[2] + f[3] * f[3]) * inv)
    out = [f[direction]]
    for member in (1, 2, 3):
        term = f[member] * speed
        out.append(term + pressure if member == direction else term)
    out.append((f[4] + pressure) * speed)
    return out


def step_kernel(
    nc, nz, state, step_size, radius, coeff, d_cells, d_weights, d_group, cells, out,
    packed, left, acc, got, packets, places, full, slab, fringed, local, own, lin, lout, rin, rout, done, back, inv_j, inv_i, lhs, coef,
    fx_send, fx_recv, pk_send, pk_recv, pl_send, pl_recv, tr_send, tr_recv, ya_send, ya_recv, zh_send, zh_recv, sc_send, sc_recv, yb_send, yb_recv,
):
    _, nj, ni = state.shape
    quarter = nj // NY
    tall = quarter + 2 * PAD
    blocks = quarter // ROWS
    chunks = blocks * NV
    slots = packed.shape[1]
    me = lax.axis_index("comp")
    panel = lax.axis_index("panel")
    z, y = panel // NY, panel % NY
    low, high = (z + nz - 1) % nz, (z + 1) % nz

    def at(comp, z_, y_):
        return (comp, z_ * NY + y_)

    barrier = pltpu.get_barrier_semaphore()
    for d in range(1, nc):
        pl.semaphore_signal(barrier, inc=1, device_id=at((me + d) % nc, z, y), device_id_type=MESH)
    for d in range(1, NY):
        pl.semaphore_signal(barrier, inc=1, device_id=at(me, z, (y + d) % NY), device_id_type=MESH)
    for q in range(NY):
        pl.semaphore_signal(barrier, inc=1, device_id=at(me, low, q), device_id_type=MESH)
        pl.semaphore_signal(barrier, inc=1, device_id=at(me, high, q), device_id_type=MESH)
    pl.semaphore_wait(barrier, nc - 1 + NY - 1 + 2 * NY)

    def quarter_copy(v, d):
        to = (y + d) % NY
        return pltpu.make_async_remote_copy(
            src_ref=full.at[v, pl.ds(pl.multiple_of(to * quarter, 8), tall), :],
            dst_ref=slab.at[2 + y, v],
            send_sem=ya_send.at[v, d],
            recv_sem=ya_recv.at[v, d],
            device_id=at(me, z, to),
            device_id_type=MESH,
        )

    def halo_copy(v, side):
        return pltpu.make_async_remote_copy(
            src_ref=slab.at[pl.ds(4 - 2 * side, 2), v, pl.ds(PAD, quarter), :],
            dst_ref=slab.at[pl.ds(6 * side, 2), v, pl.ds(PAD, quarter), :],
            send_sem=zh_send.at[v, side],
            recv_sem=zh_recv.at[v, side],
            device_id=at(me, (high, low)[side], y),
            device_id_type=MESH,
        )

    def local_copy(which, d):
        to = (y + d) % NY
        return pltpu.make_async_remote_copy(
            src_ref=(step_size, radius)[which].at[pl.ds(pl.multiple_of(to * quarter, 8), quarter), :],
            dst_ref=local.at[which, y],
            send_sem=tr_send.at[which, d],
            recv_sem=tr_recv.at[which, d],
            device_id=at(me, z, to),
            device_id_type=MESH,
        )

    def fringe(d):
        peer = (me + d) % nc
        return pltpu.make_async_remote_copy(
            src_ref=packed.at[:, pl.ds(pl.multiple_of(peer * 128, 128), 128)],
            dst_ref=got.at[me],
            send_sem=fx_send.at[d],
            recv_sem=fx_recv.at[d],
            device_id=at(peer, z, y),
            device_id_type=MESH,
        )

    has_low, has_high = z > 0, z < nz - 1
    up = y >= NY - 2
    beyond, beyond_at = jnp.where(up, high, low), (y + 6) % 8
    reaches = (up & has_high) | (jnp.logical_not(up) & has_low)

    def share(what, n):
        ref, send, recv = ((places, pl_send, pl_recv), (packets, pk_send, pk_recv))[what]
        slot = 2 + y if n < NY else beyond_at
        return pltpu.make_async_remote_copy(
            src_ref=ref.at[2 + y],
            dst_ref=ref.at[slot],
            send_sem=send.at[n],
            recv_sem=recv.at[slot],
            device_id=at(me, z, (y + n) % NY) if n < NY else at(me, beyond, n - NY),
            device_id_type=MESH,
        )

    def share_start(what):
        for n in range(1, NY):
            share(what, n).start()

        @pl.when(reaches)
        def _():
            for n in range(NY, 2 * NY):
                share(what, n).start()

    def share_sent(what):
        for n in range(1, NY):
            share(what, n).wait_send()

        @pl.when(reaches)
        def _():
            for n in range(NY, 2 * NY):
                share(what, n).wait_send()

    def share_came(what, slot):
        ref, send, recv = ((places, pl_send, pl_recv), (packets, pk_send, pk_recv))[what]
        pltpu.make_async_remote_copy(
            src_ref=ref.at[slot],
            dst_ref=ref.at[slot],
            send_sem=send.at[0],
            recv_sem=recv.at[slot],
            device_id=at(me, z, (y + 1) % NY),
            device_id_type=MESH,
        ).wait_recv()

    for v in range(NV):
        full[v, :PAD] = jnp.zeros((PAD, ni), F32)
        full[v, PAD + nj :] = jnp.zeros((PAD, ni), F32)
        full[v, PAD : PAD + nj] = state[v]
        for d in range(1, NY):
            quarter_copy(v, d).start()
    places[2 + y] = cells[...]
    share_start(0)
    for v in range(NV):
        slab[2 + y, v] = full[v, pl.ds(pl.multiple_of(y * quarter, 8), tall), :]
    mine = pl.ds(pl.multiple_of(y * quarter, 8), quarter)
    local[0, y] = step_size[mine, :]
    local[1, y] = radius[mine, :]

    h2 = jnp.full((8, 128), coeff[0, 2], F32)
    base = (z * NY - 2).astype(F32)
    k_near = inverse_entries(
        h2,
        nz * NY,
        jnp.maximum(iota((8, 128), 0).astype(F32) + base, 0.0),
        jnp.maximum(iota((8, 128), 1).astype(F32) + base, 0.0),
    )

    def entry(a, b):
        return k_near[a : a + 1, b : b + 1]

    for q in range(4):
        for l in range(4):
            coef[q * 4 + l] = entry(2 + q, 2 + l)[0, 0]
    for side, first in ((0, 0), (1, 6)):
        a, b, d = entry(first, first), entry(first, first + 1), entry(first + 1, first + 1)
        det = 1.0 / (a * d - b * b)
        edge = (z == 0) if side == 0 else (z == nz - 1)
        for q in range(4):
            s, t = entry(2 + q, first), entry(2 + q, first + 1)
            coef[16 + side * 8 + q * 2] = jnp.where(edge, 0.0, ((s * d - t * b) * det)[0, 0])
            coef[16 + side * 8 + q * 2 + 1] = jnp.where(edge, 0.0, ((t * a - s * b) * det)[0, 0])

    for ref, length, which in ((inv_j, nj, 1), (inv_i, ni, 0)):
        ref[...] = inverse_entries(
            jnp.full((1, 1), coeff[0, which], F32),
            length,
            iota((length, 1), 0).astype(F32),
            iota((1, length), 1).astype(F32),
        )

    donors(state, d_cells, d_weights, d_group, packed, left, acc)
    for d in range(1, nc):
        fringe(d).start()
    got[me] = packed[:, pl.ds(pl.multiple_of(me * 128, 128), 128)]
    for v in range(NV):
        for d in range(1, NY):
            quarter_copy(v, d).wait_recv()

        @pl.when(has_high)
        def _():
            halo_copy(v, 0).start()

        @pl.when(has_low)
        def _():
            halo_copy(v, 1).start()

    for d in range(1, nc):
        fringe(d).wait_recv()
    packets[2 + y] = jnp.concatenate([got[g] for g in range(nc)], axis=1)
    share_start(1)
    for which in range(2):
        for d in range(1, NY):
            local_copy(which, d).start()

    dims = (((1,), (1,)), ((), ()))

    def place(n, carry):
        l = (n + 2) % 8
        here = ((l >= 2) | has_low) & ((l < 6) | has_high)

        @pl.when(here & (l != 2 + y))
        def _():
            share_came(0, l)
            share_came(1, l)

        for side, first in ((0, 0), (1, 6)):

            @pl.when(here & (l == first))
            def _():
                for v in range(NV):
                    halo_copy(v, side).wait_recv()

        @pl.when(jnp.logical_not(here))
        def _():
            fringed[l] = jnp.zeros((NV, tall, ni), F32)

        @pl.when(here)
        def _():
            where, values = places[l], packets[l]
            cell = jnp.concatenate([where[g : g + 1, :] for g in range(nc)], axis=1)
            row = cell // ni - (y * quarter - PAD)
            hot_i = jnp.where(iota((ni, slots), 0) == cell % ni, 1.0, 0.0).astype(BF16)
            hot_j = jnp.where(iota((tall, slots), 0) == row, 1.0, 0.0).astype(BF16)
            split = [part.astype(F32) for part in parts(values)]

            def rows_of(line):
                sixteen = jnp.broadcast_to(line, (16, slots)).astype(BF16)
                return hot_j * jnp.concatenate([sixteen] * (tall // 16), axis=0)

            for v in range(NV):
                for k in range(3):
                    lhs[(3 * v + k) * tall : (3 * v + k + 1) * tall, :] = rows_of(split[k][v : v + 1])
            lhs[3 * NV * tall :, :] = rows_of(values[NV : NV + 1])
            put = lax.dot_general(lhs[...], hot_i, dims, preferred_element_type=F32)
            filled = put[3 * NV * tall :] > 0.5
            for v in range(NV):
                hi, mid, lo = (put[(3 * v + k) * tall : (3 * v + k + 1) * tall] for k in range(3))
                fringed[l, v] = jnp.where(filled, hi + mid + lo, slab[l, v])

        return carry

    lax.fori_loop(0, 8, place, 0)
    for which in range(2):
        for d in range(1, NY):
            local_copy(which, d).wait_recv()

    lane = iota((ROWS, ni), 1)
    for rb in range(blocks):
        top = PAD + rb * ROWS

        def layer(l, carry):
            def load(dl, dj):
                return [fringed[2 + l + dl, v, top + dj : top + dj + ROWS, :] for v in range(NV)]

            here = load(0, 0)

            def shifted(by):
                keep = (lane + by >= 0) & (lane + by < ni)
                return [jnp.where(keep, pltpu.roll(f, (-by) % ni, 1), 0.0) for f in here]

            convect, near, far = None, None, None
            for direction, look in (
                (1, shifted),
                (2, lambda by: load(0, by)),
                (3, lambda by: load(by, 0)),
            ):
                ahead, behind = look(1), look(-1)
                diff = [a - b for a, b in zip(flux(ahead, direction), flux(behind, direction))]
                one = [a + b for a, b in zip(ahead, behind)]
                two = [a + b for a, b in zip(look(2), look(-2))]
                convect = diff if convect is None else [a + b for a, b in zip(convect, diff)]
                near = one if near is None else [a + b for a, b in zip(near, one)]
                far = two if far is None else [a + b for a, b in zip(far, two)]
            dt = local[0, l, rb * ROWS : (rb + 1) * ROWS, :]
            spread = 0.0625 * local[1, l, rb * ROWS : (rb + 1) * ROWS, :]
            rhs = []
            for v in range(NV):
                smooth = far[v] - 4.0 * near[v] + 18.0 * here[v]
                rhs.append(dt * (-0.5 * convect[v] - spread * smooth))
            rhs = jnp.dot(
                jnp.concatenate(rhs, axis=0),
                inv_i[...],
                preferred_element_type=F32,
                precision=lax.Precision.HIGHEST,
            )
            for v in range(NV):
                done[l, rb * NV + v] = rhs[v * ROWS : (v + 1) * ROWS]
            return carry

        lax.fori_loop(0, NY, layer, 0)

        def block(v, carry):
            t = rb * NV + v
            rhs = [done[l, t] for l in range(NY)]
            for q in range(NY):
                own[q, t] = (
                    coef[q * 4] * rhs[0]
                    + coef[q * 4 + 1] * rhs[1]
                    + coef[q * 4 + 2] * rhs[2]
                    + coef[q * 4 + 3] * rhs[3]
                )
            return carry

        lax.fori_loop(0, NV, block, 0)

    @pl.when(z == 0)
    def _():
        lin[...] = jnp.zeros_like(lin)

    @pl.when(z == nz - 1)
    def _():
        rin[...] = jnp.zeros_like(rin)

    def pass_on(t, side):
        return pltpu.make_async_remote_copy(
            src_ref=(lout, rout)[side].at[t],
            dst_ref=(lin, rin)[side].at[t],
            send_sem=sc_send.at[side, t],
            recv_sem=sc_recv.at[side, t],
            device_id=at(me, (high, low)[side], y),
            device_id_type=MESH,
        )

    def home(rb, q, source):
        run = pl.ds(rb * NV, NV)
        return pltpu.make_async_remote_copy(
            src_ref=done.at[q, run],
            dst_ref=back.at[source, run],
            send_sem=yb_send.at[rb, q],
            recv_sem=yb_recv.at[rb, source],
            device_id=at(me, z, q),
            device_id_type=MESH,
        )

    def scan_step(t, side):
        starts, ends = (z > 0, z < nz - 1) if side == 0 else (z < nz - 1, z > 0)
        came, gone = ((lin, lout), (rin, rout))[side]

        @pl.when(starts)
        def _():
            pass_on(t, side).wait_recv()

        @pl.when(ends)
        def _():
            first, second = came[t, 0], came[t, 1]
            for m in range(2):
                q = 2 + m if side == 0 else m
                at_q = 16 + side * 8 + q * 2
                gone[t, m] = own[q, t] + coef[at_q] * first + coef[at_q + 1] * second
            pass_on(t, side).start()

    def finish(rb):
        def one(v, carry):
            t = rb * NV + v
            l0, l1, r0, r1 = lin[t, 0], lin[t, 1], rin[t, 0], rin[t, 1]
            for q in range(NY):
                done[q, t] = (
                    own[q, t]
                    + (coef[16 + q * 2] * l0 + coef[17 + q * 2] * l1)
                    + (coef[24 + q * 2] * r0 + coef[25 + q * 2] * r1)
                )
            return carry

        lax.fori_loop(0, NV, one, 0)
        for q in range(NY):

            @pl.when(y == q)
            def _():
                back[q, rb * NV : (rb + 1) * NV] = done[q, rb * NV : (rb + 1) * NV]

            @pl.when(y != q)
            def _():
                home(rb, q, y).start()

    lag = jnp.clip(LAG * (nz - 1 - 2 * z), -chunks, chunks)
    l_from, r_from = jnp.maximum(-lag, 0), jnp.maximum(lag, 0)
    last = jnp.maximum(l_from, r_from)

    def tick(s, carry):
        for side, t in enumerate((s - l_from, s - r_from)):

            @pl.when((t >= 0) & (t < chunks))
            def _():
                scan_step(t, side)

        for rb in range(blocks):

            @pl.when(s == last + (rb + 1) * NV - 1)
            def _():
                finish(rb)

        return carry

    lax.fori_loop(0, last + chunks, tick, 0)

    for rb in range(blocks):
        for s in range(NY):

            @pl.when(y != s)
            def _():
                home(rb, s, s).wait_recv()

    def solve(v, carry):
        plane = jnp.concatenate(
            [back[s, rb * NV + v] for s in range(NY) for rb in range(blocks)], axis=0
        )
        out[v] = jnp.dot(
            inv_j[...], plane, preferred_element_type=F32, precision=lax.Precision.HIGHEST
        )
        return carry

    lax.fori_loop(0, NV, solve, 0)

    share_sent(0)
    share_sent(1)
    for d in range(1, nc):
        fringe(d).wait_send()
    for d in range(1, NY):
        for which in range(2):
            local_copy(which, d).wait_send()
        for v in range(NV):
            quarter_copy(v, d).wait_send()
    for v in range(NV):

        @pl.when(z < nz - 1)
        def _():
            halo_copy(v, 0).wait_send()

        @pl.when(z > 0)
        def _():
            halo_copy(v, 1).wait_send()

    def drain(t, carry):
        @pl.when(z < nz - 1)
        def _():
            pass_on(t, 0).wait_send()

        @pl.when(z > 0)
        def _():
            pass_on(t, 1).wait_send()

        return carry

    lax.fori_loop(0, chunks, drain, 0)
    for rb in range(blocks):
        for q in range(NY):

            @pl.when(y != q)
            def _():
                home(rb, q, y).wait_send()


def vmem():
    return pl.BlockSpec(memory_space=pltpu.VMEM)


def body(nc, nz, state, time_step, radius, coeff, donor_cells, donor_weights, donor_group, recv_cells):
    _, nv, _, nj, ni = state.shape
    slots = recv_cells.shape[2] * recv_cells.shape[3]
    don = donor_cells.shape[3]
    quarter = nj // NY
    chunks = quarter // ROWS * NV
    field = state.reshape(nv, nj, ni)
    dma = pltpu.SemaphoreType.DMA
    delta = pl.pallas_call(
        functools.partial(step_kernel, nc, nz),
        out_shape=jax.ShapeDtypeStruct((nv, nj, ni), F32),
        in_specs=[vmem()] * 3 + [pl.BlockSpec(memory_space=pltpu.SMEM)] + [vmem()] * 4,
        out_specs=vmem(),
        scratch_shapes=[
            pltpu.VMEM((8, slots), F32),
            pltpu.VMEM((nv * nj, 3 * ni), BF16),
            pltpu.VMEM((nv, 8, don), F32),
            pltpu.VMEM((nc, 8, 128), F32),
            pltpu.VMEM((2 * NY, 8, slots), F32),
            pltpu.VMEM((2 * NY,) + recv_cells.shape[2:], jnp.int32),
            pltpu.VMEM((nv, nj + 2 * PAD, ni), F32),
            pltpu.VMEM((2 * NY, nv, quarter + 2 * PAD, ni), F32),
            pltpu.VMEM((2 * NY, nv, quarter + 2 * PAD, ni), F32),
            pltpu.VMEM((2, NY, quarter, ni), F32),
            pltpu.VMEM((NY, chunks, ROWS, ni), F32),
            pltpu.VMEM((chunks, 2, ROWS, ni), F32),
            pltpu.VMEM((chunks, 2, ROWS, ni), F32),
            pltpu.VMEM((chunks, 2, ROWS, ni), F32),
            pltpu.VMEM((chunks, 2, ROWS, ni), F32),
            pltpu.VMEM((NY, chunks, ROWS, ni), F32),
            pltpu.VMEM((NY, chunks, ROWS, ni), F32),
            pltpu.VMEM((nj, nj), F32),
            pltpu.VMEM((ni, ni), F32),
            pltpu.VMEM(((3 * nv + 1) * (quarter + 2 * PAD), slots), BF16),
            pltpu.SMEM((32,), F32),
            dma((nc,)), dma((nc,)),
            dma((2 * NY,)), dma((2 * NY,)),
            dma((2 * NY,)), dma((2 * NY,)),
            dma((2, NY)), dma((2, NY)),
            dma((nv, NY)), dma((nv, NY)),
            dma((nv, 2)), dma((nv, 2)),
            dma((2, chunks)), dma((2, chunks)),
            dma((quarter // ROWS, NY)), dma((quarter // ROWS, NY)),
        ],
        compiler_params=pltpu.CompilerParams(
            collective_id=0, has_side_effects=True, vmem_limit_bytes=48 * 2**20
        ),
        name="step",
    )(
        field,
        time_step.reshape(nj, ni),
        radius.reshape(nj, ni),
        coeff,
        donor_cells.reshape(donor_cells.shape[2:]),
        donor_weights.reshape(donor_weights.shape[2:]),
        donor_group.reshape(don, 1),
        recv_cells.reshape(recv_cells.shape[2:]),
    )
    return delta.reshape(state.shape)


def solution(mesh):
    slabs = P("comp", "panel", None, None)
    whole = P("comp", None, "panel", None, None)
    return jax.shard_map(
        functools.partial(body, mesh.shape["comp"], mesh.shape["panel"] // NY),
        mesh=mesh,
        in_specs=(whole, slabs, slabs, P("comp", None), slabs, slabs, slabs, slabs),
        out_specs=whole,
        check_vma=False,
    )
```

```python
import functools

import jax
import jax.numpy as jnp
from jax import lax
from jax.experimental import pallas as pl
from jax.experimental.pallas import tpu as pltpu
from jax.sharding import PartitionSpec as P

MESH = pl.DeviceIdType.MESH
F32, BF16 = jnp.float32, jnp.bfloat16
NV = 5
NY = 4
PAD = 8
LAG = 6
ROWS = 16


def parts(x):
    hi = x.astype(BF16)
    return hi, (x - hi.astype(F32)).astype(BF16)


def product(a, b):
    return (
        jnp.dot(a[0], b[0], preferred_element_type=F32)
        + jnp.dot(a[0], b[1], preferred_element_type=F32)
        + jnp.dot(a[1], b[0], preferred_element_type=F32)
    )


def inverse_entries(h, length, i, j):
    root = jnp.sqrt(16.0 - 8.0 / h)
    m1, m2 = (8.0 / h) / (4.0 + root), 4.0 + root
    n = float(length)

    def green(m, a, b):
        s = 0.5 * jnp.sqrt(m)
        t = 2.0 * jnp.log(s + jnp.sqrt(1.0 + s * s))
        d = jnp.abs(a - b)
        top = (
            jnp.exp(-t * d)
            - jnp.exp(-t * (a + b + 2.0))
            - jnp.exp(-t * (2.0 * n - a - b))
            + jnp.exp(-t * (2.0 * n + 2.0 - d))
        )
        two_sinh = jnp.exp(t) - jnp.exp(-t)
        return top / (two_sinh * (1.0 - jnp.exp(-2.0 * t * (n + 1.0))))

    def smooth(a, b):
        return (8.0 / h) * (green(m1, a, b) - green(m2, a, b)) / (m2 - m1)

    zero = jnp.zeros_like(h)
    corner, across = smooth(zero, zero), smooth(zero, zero + (n - 1.0))
    even_scale = 0.5 / (8.0 / h + corner + across)
    odd_scale = 0.5 / (8.0 / h + corner - across)
    i0, i1 = smooth(i, zero), smooth(i, zero + (n - 1.0))
    j0, j1 = smooth(j, zero), smooth(j, zero + (n - 1.0))
    return (
        smooth(i, j)
        - even_scale * (i0 + i1) * (j0 + j1)
        - odd_scale * (i0 - i1) * (j0 - j1)
    )


def iota(shape, axis):
    return lax.broadcasted_iota(jnp.int32, shape, axis)


def donors(state, cells, weights, group, packed, left, acc):
    nv, nj, ni = state.shape
    n_c, don = cells.shape
    count = packed.shape[1] // 128
    width = min(256, don)
    flat = state[...].reshape(nv * nj, ni)
    for k, part in enumerate(parts(flat)):
        left[:, k * ni : (k + 1) * ni] = part
    acc[...] = jnp.zeros_like(acc)

    for block in range(don // width):
        span = slice(block * width, (block + 1) * width)

        def one(c, carry):
            cell = cells[pl.ds(c, 1), span]
            weight = weights[pl.ds(c, 1), span]
            col = jnp.where(iota((ni, width), 0) == cell % ni, 1.0, 0.0).astype(BF16)
            got = jnp.dot(
                left[...], jnp.concatenate([col, col], axis=0), preferred_element_type=F32
            )
            row = jnp.where(iota((nj, width), 0) == cell // ni, weight, 0.0)
            for v in range(nv):
                term = got[v * nj : (v + 1) * nj] * row
                acc[v, :, span] += jnp.sum(term.reshape(nj // 8, 8, width), axis=0)
            return carry

        lax.fori_loop(0, n_c, one, 0)

    values = [jnp.sum(acc[v], axis=0, keepdims=True) for v in range(nv)]
    values = jnp.concatenate(
        values + [jnp.ones((1, don), F32), jnp.zeros((8 - nv - 1, don), F32)], axis=0
    )
    mine = group[...]
    hot = jnp.where(iota((16, don), 0) == mine, 1.0, 0.0)
    before = jnp.where(iota((don, don), 0) < iota((don, don), 1), 1.0, 0.0).astype(BF16)
    ahead = jnp.dot(hot.astype(BF16), before, preferred_element_type=F32)
    target = mine * 128 + jnp.sum(hot * ahead, axis=0, keepdims=True).astype(jnp.int32)
    place = jnp.where(iota((count * 128, don), 0) == target, 1.0, 0.0).astype(BF16)
    dims = (((1,), (1,)), ((), ()))
    hi, lo = parts(values)
    packed[...] = lax.dot_general(hi, place, dims, preferred_element_type=F32) + lax.dot_general(
        lo, place, dims, preferred_element_type=F32
    )


def flux(f, direction):
    rho = jnp.where(f[0] > 0.0, f[0], 1.0)
    inv = 1.0 / rho
    speed = f[direction] * inv
    pressure = 0.4 * (f[4] - 0.5 * (f[1] * f[1] + f[2] * f[2] + f[3] * f[3]) * inv)
    out = [f[direction]]
    for member in (1, 2, 3):
        term = f[member] * speed
        out.append(term + pressure if member == direction else term)
    out.append((f[4] + pressure) * speed)
    return out


def step_kernel(
    nc, nz, state, step_size, radius, coeff, d_cells, d_weights, d_group, cells, out,
    packed, left, acc, got, packets, places, full, slab, fringed, local, own, lin, lout, rin, rout, done, back, inv_j, inv_i, lhs, coef,
    fx_send, fx_recv, pk_send, pk_recv, pl_send, pl_recv, tr_send, tr_recv, ya_send, ya_recv, zh_send, zh_recv, sc_send, sc_recv, yb_send, yb_recv,
):
    _, nj, ni = state.shape
    quarter = nj // NY
    tall = quarter + 2 * PAD
    blocks = quarter // ROWS
    chunks = blocks * NV
    slots = packed.shape[1]
    me = lax.axis_index("comp")
    panel = lax.axis_index("panel")
    z, y = panel // NY, panel % NY
    low, high = (z + nz - 1) % nz, (z + 1) % nz

    def at(comp, z_, y_):
        return (comp, z_ * NY + y_)

    barrier = pltpu.get_barrier_semaphore()
    for d in range(1, nc):
        pl.semaphore_signal(barrier, inc=1, device_id=at((me + d) % nc, z, y), device_id_type=MESH)
    for d in range(1, NY):
        pl.semaphore_signal(barrier, inc=1, device_id=at(me, z, (y + d) % NY), device_id_type=MESH)
    for q in range(NY):
        pl.semaphore_signal(barrier, inc=1, device_id=at(me, low, q), device_id_type=MESH)
        pl.semaphore_signal(barrier, inc=1, device_id=at(me, high, q), device_id_type=MESH)
    pl.semaphore_wait(barrier, nc - 1 + NY - 1 + 2 * NY)

    def quarter_copy(v, d):
        to = (y + d) % NY
        return pltpu.make_async_remote_copy(
            src_ref=full.at[v, pl.ds(pl.multiple_of(to * quarter, 8), tall), :],
            dst_ref=slab.at[2 + y, v],
            send_sem=ya_send.at[v, d],
            recv_sem=ya_recv.at[v, d],
            device_id=at(me, z, to),
            device_id_type=MESH,
        )

    def halo_copy(v, side):
        return pltpu.make_async_remote_copy(
            src_ref=slab.at[pl.ds(4 - 2 * side, 2), v, pl.ds(PAD, quarter), :],
            dst_ref=slab.at[pl.ds(6 * side, 2), v, pl.ds(PAD, quarter), :],
            send_sem=zh_send.at[v, side],
            recv_sem=zh_recv.at[v, side],
            device_id=at(me, (high, low)[side], y),
            device_id_type=MESH,
        )

    def local_copy(which, d):
        to = (y + d) % NY
        return pltpu.make_async_remote_copy(
            src_ref=(step_size, radius)[which].at[pl.ds(pl.multiple_of(to * quarter, 8), quarter), :],
            dst_ref=local.at[which, y],
            send_sem=tr_send.at[which, d],
            recv_sem=tr_recv.at[which, d],
            device_id=at(me, z, to),
            device_id_type=MESH,
        )

    def fringe(d):
        peer = (me + d) % nc
        return pltpu.make_async_remote_copy(
            src_ref=packed.at[:, pl.ds(pl.multiple_of(peer * 128, 128), 128)],
            dst_ref=got.at[me],
            send_sem=fx_send.at[d],
            recv_sem=fx_recv.at[d],
            device_id=at(peer, z, y),
            device_id_type=MESH,
        )

    has_low, has_high = z > 0, z < nz - 1
    up = y >= NY - 2
    beyond, beyond_at = jnp.where(up, high, low), (y + 6) % 8
    reaches = (up & has_high) | (jnp.logical_not(up) & has_low)

    def share(what, n):
        ref, send, recv = ((places, pl_send, pl_recv), (packets, pk_send, pk_recv))[what]
        slot = 2 + y if n < NY else beyond_at
        return pltpu.make_async_remote_copy(
            src_ref=ref.at[2 + y],
            dst_ref=ref.at[slot],
            send_sem=send.at[n],
            recv_sem=recv.at[slot],
            device_id=at(me, z, (y + n) % NY) if n < NY else at(me, beyond, n - NY),
            device_id_type=MESH,
        )

    def share_start(what):
        for n in range(1, NY):
            share(what, n).start()

        @pl.when(reaches)
        def _():
            for n in range(NY, 2 * NY):
                share(what, n).start()

    def share_sent(what):
        for n in range(1, NY):
            share(what, n).wait_send()

        @pl.when(reaches)
        def _():
            for n in range(NY, 2 * NY):
                share(what, n).wait_send()

    def share_came(what, slot):
        ref, send, recv = ((places, pl_send, pl_recv), (packets, pk_send, pk_recv))[what]
        pltpu.make_async_remote_copy(
            src_ref=ref.at[slot],
            dst_ref=ref.at[slot],
            send_sem=send.at[0],
            recv_sem=recv.at[slot],
            device_id=at(me, z, (y + 1) % NY),
            device_id_type=MESH,
        ).wait_recv()

    for v in range(NV):
        full[v, :PAD] = jnp.zeros((PAD, ni), F32)
        full[v, PAD + nj :] = jnp.zeros((PAD, ni), F32)
        full[v, PAD : PAD + nj] = state[v]
        for d in range(1, NY):
            quarter_copy(v, d).start()
    places[2 + y] = cells[...]
    share_start(0)
    for which in range(2):
        for d in range(1, NY):
            local_copy(which, d).start()
    for v in range(NV):
        slab[2 + y, v] = full[v, pl.ds(pl.multiple_of(y * quarter, 8), tall), :]
    mine = pl.ds(pl.multiple_of(y * quarter, 8), quarter)
    local[0, y] = step_size[mine, :]
    local[1, y] = radius[mine, :]

    h2 = jnp.full((8, 128), coeff[0, 2], F32)
    base = (z * NY - 2).astype(F32)
    k_near = inverse_entries(
        h2,
        nz * NY,
        jnp.maximum(iota((8, 128), 0).astype(F32) + base, 0.0),
        jnp.maximum(iota((8, 128), 1).astype(F32) + base, 0.0),
    )

    def entry(a, b):
        return k_near[a : a + 1, b : b + 1]

    for q in range(4):
        for l in range(4):
            coef[q * 4 + l] = entry(2 + q, 2 + l)[0, 0]
    for side, first in ((0, 0), (1, 6)):
        a, b, d = entry(first, first), entry(first, first + 1), entry(first + 1, first + 1)
        det = 1.0 / (a * d - b * b)
        edge = (z == 0) if side == 0 else (z == nz - 1)
        for q in range(4):
            s, t = entry(2 + q, first), entry(2 + q, first + 1)
            coef[16 + side * 8 + q * 2] = jnp.where(edge, 0.0, ((s * d - t * b) * det)[0, 0])
            coef[16 + side * 8 + q * 2 + 1] = jnp.where(edge, 0.0, ((t * a - s * b) * det)[0, 0])

    for ref, length, which in ((inv_j, nj, 1), (inv_i, ni, 0)):
        ref[0], ref[1] = parts(
            inverse_entries(
                jnp.full((1, 1), coeff[0, which], F32),
                length,
                iota((length, 1), 0).astype(F32),
                iota((1, length), 1).astype(F32),
            )
        )

    donors(state, d_cells, d_weights, d_group, packed, left, acc)
    for d in range(1, nc):
        fringe(d).start()
    got[me] = packed[:, pl.ds(pl.multiple_of(me * 128, 128), 128)]
    for v in range(NV):
        for d in range(1, NY):
            quarter_copy(v, d).wait_recv()

        @pl.when(has_high)
        def _():
            halo_copy(v, 0).start()

        @pl.when(has_low)
        def _():
            halo_copy(v, 1).start()

    for d in range(1, nc):
        fringe(d).wait_recv()
    packets[2 + y] = jnp.concatenate([got[g] for g in range(nc)], axis=1)
    share_start(1)

    dims = (((1,), (1,)), ((), ()))

    def place(n, carry):
        l = (n + 2) % 8
        here = ((l >= 2) | has_low) & ((l < 6) | has_high)

        @pl.when(here & (l != 2 + y))
        def _():
            share_came(0, l)
            share_came(1, l)

        for side, first in ((0, 0), (1, 6)):

            @pl.when(here & (l == first))
            def _():
                for v in range(NV):
                    halo_copy(v, side).wait_recv()

        @pl.when(jnp.logical_not(here))
        def _():
            fringed[l] = jnp.zeros((NV, tall, ni), F32)

        @pl.when(here)
        def _():
            where, values = places[l], packets[l]
            cell = jnp.concatenate([where[g : g + 1, :] for g in range(nc)], axis=1)
            row = cell // ni - (y * quarter - PAD)
            hot_i = jnp.where(iota((ni, slots), 0) == cell % ni, 1.0, 0.0).astype(BF16)
            hot_j = jnp.where(iota((tall, slots), 0) == row, 1.0, 0.0).astype(BF16)
            split = [part.astype(F32) for part in parts(values)]

            def rows_of(line):
                sixteen = jnp.broadcast_to(line, (16, slots)).astype(BF16)
                return hot_j * jnp.concatenate([sixteen] * (tall // 16), axis=0)

            for v in range(NV):
                for k in range(2):
                    lhs[(2 * v + k) * tall : (2 * v + k + 1) * tall, :] = rows_of(split[k][v : v + 1])
            lhs[2 * NV * tall :, :] = rows_of(values[NV : NV + 1])
            put = lax.dot_general(lhs[...], hot_i, dims, preferred_element_type=F32)
            filled = put[2 * NV * tall :] > 0.5
            for v in range(NV):
                hi, lo = (put[(2 * v + k) * tall : (2 * v + k + 1) * tall] for k in range(2))
                fringed[l, v] = jnp.where(filled, hi + lo, slab[l, v])

        return carry

    lax.fori_loop(0, 8, place, 0)
    for which in range(2):
        for d in range(1, NY):
            local_copy(which, d).wait_recv()

    def pass_on(t, side):
        return pltpu.make_async_remote_copy(
            src_ref=(lout, rout)[side].at[t],
            dst_ref=(lin, rin)[side].at[t],
            send_sem=sc_send.at[side, t],
            recv_sem=sc_recv.at[side, t],
            device_id=at(me, (high, low)[side], y),
            device_id_type=MESH,
        )

    @pl.when(z == 0)
    def _():
        lin[...] = jnp.zeros_like(lin)

    @pl.when(z == nz - 1)
    def _():
        rin[...] = jnp.zeros_like(rin)

    lane = iota((ROWS, ni), 1)
    for rb in range(blocks):
        top = PAD + rb * ROWS

        def layer(l, carry):
            def load(dl, dj):
                return [fringed[2 + l + dl, v, top + dj : top + dj + ROWS, :] for v in range(NV)]

            here = load(0, 0)

            def shifted(by):
                keep = (lane + by >= 0) & (lane + by < ni)
                return [jnp.where(keep, pltpu.roll(f, (-by) % ni, 1), 0.0) for f in here]

            convect, near, far = None, None, None
            for direction, look in (
                (1, shifted),
                (2, lambda by: load(0, by)),
                (3, lambda by: load(by, 0)),
            ):
                ahead, behind = look(1), look(-1)
                diff = [a - b for a, b in zip(flux(ahead, direction), flux(behind, direction))]
                one = [a + b for a, b in zip(ahead, behind)]
                two = [a + b for a, b in zip(look(2), look(-2))]
                convect = diff if convect is None else [a + b for a, b in zip(convect, diff)]
                near = one if near is None else [a + b for a, b in zip(near, one)]
                far = two if far is None else [a + b for a, b in zip(far, two)]
            dt = local[0, l, rb * ROWS : (rb + 1) * ROWS, :]
            spread = 0.0625 * local[1, l, rb * ROWS : (rb + 1) * ROWS, :]
            rhs = []
            for v in range(NV):
                smooth = far[v] - 4.0 * near[v] + 18.0 * here[v]
                rhs.append(dt * (-0.5 * convect[v] - spread * smooth))
            for v in range(NV):
                done[l, rb * NV + v] = rhs[v]
            return carry

        lax.fori_loop(0, NY, layer, 0)

        run = slice(rb * NV, (rb + 1) * NV)
        solved = product(parts(done[:, run].reshape(NY * NV * ROWS, ni)), inv_i)
        solved = solved.reshape(NY, NV, ROWS, ni)
        for v in range(NV):
            for q in range(NY):
                own[q, rb * NV + v] = (
                    coef[q * 4] * solved[0, v]
                    + coef[q * 4 + 1] * solved[1, v]
                    + coef[q * 4 + 2] * solved[2, v]
                    + coef[q * 4 + 3] * solved[3, v]
                )

        @pl.when(z == 0)
        def _():
            for t in range(rb * NV, (rb + 1) * NV):
                lout[t] = own[2:4, t]
                pass_on(t, 0).start()

        @pl.when(z == nz - 1)
        def _():
            for t in range(rb * NV, (rb + 1) * NV):
                rout[t] = own[0:2, t]
                pass_on(t, 1).start()

    def home(rb, q, source):
        run = pl.ds(rb * NV, NV)
        return pltpu.make_async_remote_copy(
            src_ref=done.at[q, run],
            dst_ref=back.at[source, run],
            send_sem=yb_send.at[rb, q],
            recv_sem=yb_recv.at[rb, source],
            device_id=at(me, z, q),
            device_id_type=MESH,
        )

    def scan_step(t, side):
        edge, other = (z == 0, z == nz - 1) if side == 0 else (z == nz - 1, z == 0)
        came, gone = ((lin, lout), (rin, rout))[side]

        @pl.when(jnp.logical_not(edge))
        def _():
            pass_on(t, side).wait_recv()

            @pl.when(jnp.logical_not(other))
            def _():
                first, second = came[t, 0], came[t, 1]
                for m in range(2):
                    q = 2 + m if side == 0 else m
                    at_q = 16 + side * 8 + q * 2
                    gone[t, m] = own[q, t] + coef[at_q] * first + coef[at_q + 1] * second
                pass_on(t, side).start()

    def finish(rb):
        for t in range(rb * NV, (rb + 1) * NV):
            l0, l1, r0, r1 = lin[t, 0], lin[t, 1], rin[t, 0], rin[t, 1]
            for q in range(NY):
                done[q, t] = (
                    own[q, t]
                    + (coef[16 + q * 2] * l0 + coef[17 + q * 2] * l1)
                    + (coef[24 + q * 2] * r0 + coef[25 + q * 2] * r1)
                )
        for q in range(NY):

            @pl.when(y == q)
            def _():
                back[q, rb * NV : (rb + 1) * NV] = done[q, rb * NV : (rb + 1) * NV]

            @pl.when(y != q)
            def _():
                home(rb, q, y).start()

    def run_scan(side, lag):
        for s in range(lag + chunks):
            if s < chunks:
                scan_step(s, side)
            if s >= lag:
                scan_step(s - lag, 1 - side)
                if (s - lag + 1) % NV == 0:
                    finish((s - lag) // NV)

    middle = nz // 2
    near = min(LAG, chunks)
    for here, side, lag in (
        (z < middle - 1, 0, chunks),
        (z == middle - 1, 0, near),
        (z == middle, 1, near),
        (z > middle, 1, chunks),
    ):

        @pl.when(here)
        def _():
            run_scan(side, lag)

    for rb in range(blocks):
        for s in range(NY):

            @pl.when(y != s)
            def _():
                home(rb, s, s).wait_recv()

    def solve(v, carry):
        plane = jnp.concatenate(
            [back[s, rb * NV + v] for s in range(NY) for rb in range(blocks)], axis=0
        )
        out[v] = product(inv_j, parts(plane))
        return carry

    lax.fori_loop(0, NV, solve, 0)

    share_sent(0)
    share_sent(1)
    for d in range(1, nc):
        fringe(d).wait_send()
    for d in range(1, NY):
        for which in range(2):
            local_copy(which, d).wait_send()
        for v in range(NV):
            quarter_copy(v, d).wait_send()
    for v in range(NV):

        @pl.when(z < nz - 1)
        def _():
            halo_copy(v, 0).wait_send()

        @pl.when(z > 0)
        def _():
            halo_copy(v, 1).wait_send()

    def drain(t, carry):
        @pl.when(z < nz - 1)
        def _():
            pass_on(t, 0).wait_send()

        @pl.when(z > 0)
        def _():
            pass_on(t, 1).wait_send()

        return carry

    lax.fori_loop(0, chunks, drain, 0)
    for rb in range(blocks):
        for q in range(NY):

            @pl.when(y != q)
            def _():
                home(rb, q, y).wait_send()


def vmem():
    return pl.BlockSpec(memory_space=pltpu.VMEM)


def body(nc, nz, state, time_step, radius, coeff, donor_cells, donor_weights, donor_group, recv_cells):
    _, nv, _, nj, ni = state.shape
    slots = recv_cells.shape[2] * recv_cells.shape[3]
    don = donor_cells.shape[3]
    quarter = nj // NY
    chunks = quarter // ROWS * NV
    field = state.reshape(nv, nj, ni)
    dma = pltpu.SemaphoreType.DMA
    delta = pl.pallas_call(
        functools.partial(step_kernel, nc, nz),
        out_shape=jax.ShapeDtypeStruct((nv, nj, ni), F32),
        in_specs=[vmem()] * 3 + [pl.BlockSpec(memory_space=pltpu.SMEM)] + [vmem()] * 4,
        out_specs=vmem(),
        scratch_shapes=[
            pltpu.VMEM((8, slots), F32),
            pltpu.VMEM((nv * nj, 2 * ni), BF16),
            pltpu.VMEM((nv, 8, don), F32),
            pltpu.VMEM((nc, 8, 128), F32),
            pltpu.VMEM((2 * NY, 8, slots), F32),
            pltpu.VMEM((2 * NY,) + recv_cells.shape[2:], jnp.int32),
            pltpu.VMEM((nv, nj + 2 * PAD, ni), F32),
            pltpu.VMEM((2 * NY, nv, quarter + 2 * PAD, ni), F32),
            pltpu.VMEM((2 * NY, nv, quarter + 2 * PAD, ni), F32),
            pltpu.VMEM((2, NY, quarter, ni), F32),
            pltpu.VMEM((NY, chunks, ROWS, ni), F32),
            pltpu.VMEM((chunks, 2, ROWS, ni), F32),
            pltpu.VMEM((chunks, 2, ROWS, ni), F32),
            pltpu.VMEM((chunks, 2, ROWS, ni), F32),
            pltpu.VMEM((chunks, 2, ROWS, ni), F32),
            pltpu.VMEM((NY, chunks, ROWS, ni), F32),
            pltpu.VMEM((NY, chunks, ROWS, ni), F32),
            pltpu.VMEM((2, nj, nj), BF16),
            pltpu.VMEM((2, ni, ni), BF16),
            pltpu.VMEM(((2 * nv + 1) * (quarter + 2 * PAD), slots), BF16),
            pltpu.SMEM((32,), F32),
            dma((nc,)), dma((nc,)),
            dma((2 * NY,)), dma((2 * NY,)),
            dma((2 * NY,)), dma((2 * NY,)),
            dma((2, NY)), dma((2, NY)),
            dma((nv, NY)), dma((nv, NY)),
            dma((nv, 2)), dma((nv, 2)),
            dma((2, chunks)), dma((2, chunks)),
            dma((quarter // ROWS, NY)), dma((quarter // ROWS, NY)),
        ],
        compiler_params=pltpu.CompilerParams(
            collective_id=0, has_side_effects=True, vmem_limit_bytes=48 * 2**20
        ),
        name="step",
    )(
        field,
        time_step.reshape(nj, ni),
        radius.reshape(nj, ni),
        coeff,
        donor_cells.reshape(donor_cells.shape[2:]),
        donor_weights.reshape(donor_weights.shape[2:]),
        donor_group.reshape(1, don),
        recv_cells.reshape(recv_cells.shape[2:]),
    )
    return delta.reshape(state.shape)


def solution(mesh):
    slabs = P("comp", "panel", None, None)
    whole = P("comp", None, "panel", None, None)
    return jax.shard_map(
        functools.partial(body, mesh.shape["comp"], mesh.shape["panel"] // NY),
        mesh=mesh,
        in_specs=(whole, slabs, slabs, P("comp", None), slabs, slabs, slabs, slabs),
        out_specs=whole,
        check_vma=False,
    )
```

```python
import functools

import jax
import jax.numpy as jnp
from jax import lax
from jax.experimental import pallas as pl
from jax.experimental.pallas import tpu as pltpu
from jax.sharding import PartitionSpec as P

MESH = pl.DeviceIdType.MESH
F32, BF16 = jnp.float32, jnp.bfloat16
NV = 5
NY = 4
PAD = 8
LAG = 6
ROWS = 16


def parts(x):
    hi = x.astype(BF16)
    return hi, (x - hi.astype(F32)).astype(BF16)


def product(a, b):
    return (
        jnp.dot(a[0], b[0], preferred_element_type=F32)
        + jnp.dot(a[0], b[1], preferred_element_type=F32)
        + jnp.dot(a[1], b[0], preferred_element_type=F32)
    )


def inverse_entries(h, length, i, j):
    root = jnp.sqrt(16.0 - 8.0 / h)
    m1, m2 = (8.0 / h) / (4.0 + root), 4.0 + root
    n = float(length)

    def green(m, a, b):
        s = 0.5 * jnp.sqrt(m)
        t = 2.0 * jnp.log(s + jnp.sqrt(1.0 + s * s))
        d = jnp.abs(a - b)
        top = (
            jnp.exp(-t * d)
            - jnp.exp(-t * (a + b + 2.0))
            - jnp.exp(-t * (2.0 * n - a - b))
            + jnp.exp(-t * (2.0 * n + 2.0 - d))
        )
        two_sinh = jnp.exp(t) - jnp.exp(-t)
        return top / (two_sinh * (1.0 - jnp.exp(-2.0 * t * (n + 1.0))))

    def smooth(a, b):
        return (8.0 / h) * (green(m1, a, b) - green(m2, a, b)) / (m2 - m1)

    zero = jnp.zeros_like(h)
    corner, across = smooth(zero, zero), smooth(zero, zero + (n - 1.0))
    even_scale = 0.5 / (8.0 / h + corner + across)
    odd_scale = 0.5 / (8.0 / h + corner - across)
    i0, i1 = smooth(i, zero), smooth(i, zero + (n - 1.0))
    j0, j1 = smooth(j, zero), smooth(j, zero + (n - 1.0))
    return (
        smooth(i, j)
        - even_scale * (i0 + i1) * (j0 + j1)
        - odd_scale * (i0 - i1) * (j0 - j1)
    )


def iota(shape, axis):
    return lax.broadcasted_iota(jnp.int32, shape, axis)


def donors(state, cells, weights, group, packed, left, acc, between):
    nv, nj, ni = state.shape
    n_c, don = cells.shape
    count = packed.shape[1] // 128
    width = min(256, don)
    flat = state[...].reshape(nv * nj, ni)
    for k, part in enumerate(parts(flat)):
        left[:, k * ni : (k + 1) * ni] = part
    acc[...] = jnp.zeros_like(acc)

    for block in range(don // width):
        span = slice(block * width, (block + 1) * width)

        def one(c, carry):
            cell = cells[pl.ds(c, 1), span]
            weight = weights[pl.ds(c, 1), span]
            col = jnp.where(iota((ni, width), 0) == cell % ni, 1.0, 0.0).astype(BF16)
            got = jnp.dot(
                left[...], jnp.concatenate([col, col], axis=0), preferred_element_type=F32
            )
            row = jnp.where(iota((nj, width), 0) == cell // ni, weight, 0.0)
            for v in range(nv):
                term = got[v * nj : (v + 1) * nj] * row
                acc[v, :, span] += jnp.sum(term.reshape(nj // 8, 8, width), axis=0)
            return carry

        for half in range(2):
            lax.fori_loop(half * n_c // 2, (half + 1) * n_c // 2, one, 0)
            between()

    values = [jnp.sum(acc[v], axis=0, keepdims=True) for v in range(nv)]
    values = jnp.concatenate(
        values + [jnp.ones((1, don), F32), jnp.zeros((8 - nv - 1, don), F32)], axis=0
    )
    mine = group[...]
    hot = jnp.where(iota((16, don), 0) == mine, 1.0, 0.0)
    before = jnp.where(iota((don, don), 0) < iota((don, don), 1), 1.0, 0.0).astype(BF16)
    ahead = jnp.dot(hot.astype(BF16), before, preferred_element_type=F32)
    target = mine * 128 + jnp.sum(hot * ahead, axis=0, keepdims=True).astype(jnp.int32)
    place = jnp.where(iota((count * 128, don), 0) == target, 1.0, 0.0).astype(BF16)
    dims = (((1,), (1,)), ((), ()))
    hi, lo = parts(values)
    packed[...] = lax.dot_general(hi, place, dims, preferred_element_type=F32) + lax.dot_general(
        lo, place, dims, preferred_element_type=F32
    )


def flux(f, direction):
    rho = jnp.where(f[0] > 0.0, f[0], 1.0)
    inv = 1.0 / rho
    speed = f[direction] * inv
    pressure = 0.4 * (f[4] - 0.5 * (f[1] * f[1] + f[2] * f[2] + f[3] * f[3]) * inv)
    out = [f[direction]]
    for member in (1, 2, 3):
        term = f[member] * speed
        out.append(term + pressure if member == direction else term)
    out.append((f[4] + pressure) * speed)
    return out


def step_kernel(
    nc, nz, state, step_size, radius, coeff, d_cells, d_weights, d_group, cells, out,
    packed, left, acc, got, packets, places, full, slab, fringed, local, own, lin, lout, rin, rout, done, back, inv_j, inv_i, lhs, coef,
    fx_send, fx_recv, pk_send, pk_recv, pl_send, pl_recv, tr_send, tr_recv, ya_send, ya_recv, zh_send, zh_recv, sc_send, sc_recv, yb_send, yb_recv,
):
    _, nj, ni = state.shape
    quarter = nj // NY
    tall = quarter + 2 * PAD
    blocks = quarter // ROWS
    chunks = blocks * NV
    slots = packed.shape[1]
    me = lax.axis_index("comp")
    panel = lax.axis_index("panel")
    z, y = panel // NY, panel % NY
    low, high = (z + nz - 1) % nz, (z + 1) % nz

    def at(comp, z_, y_):
        return (comp, z_ * NY + y_)

    barrier = pltpu.get_barrier_semaphore()
    for d in range(1, nc):
        pl.semaphore_signal(barrier, inc=1, device_id=at((me + d) % nc, z, y), device_id_type=MESH)
    for d in range(1, NY):
        pl.semaphore_signal(barrier, inc=1, device_id=at(me, z, (y + d) % NY), device_id_type=MESH)
    for q in range(NY):
        pl.semaphore_signal(barrier, inc=1, device_id=at(me, low, q), device_id_type=MESH)
        pl.semaphore_signal(barrier, inc=1, device_id=at(me, high, q), device_id_type=MESH)
    pl.semaphore_wait(barrier, nc - 1 + NY - 1 + 2 * NY)

    def quarter_copy(v, d):
        to = (y + d) % NY
        return pltpu.make_async_remote_copy(
            src_ref=full.at[v, pl.ds(pl.multiple_of(to * quarter, 8), tall), :],
            dst_ref=slab.at[2 + y, v],
            send_sem=ya_send.at[v, d],
            recv_sem=ya_recv.at[v, d],
            device_id=at(me, z, to),
            device_id_type=MESH,
        )

    def halo_copy(v, side):
        return pltpu.make_async_remote_copy(
            src_ref=slab.at[pl.ds(4 - 2 * side, 2), v, pl.ds(PAD, quarter), :],
            dst_ref=slab.at[pl.ds(6 * side, 2), v, pl.ds(PAD, quarter), :],
            send_sem=zh_send.at[v, side],
            recv_sem=zh_recv.at[v, side],
            device_id=at(me, (high, low)[side], y),
            device_id_type=MESH,
        )

    def local_copy(which, d):
        to = (y + d) % NY
        return pltpu.make_async_remote_copy(
            src_ref=(step_size, radius)[which].at[pl.ds(pl.multiple_of(to * quarter, 8), quarter), :],
            dst_ref=local.at[which, y],
            send_sem=tr_send.at[which, d],
            recv_sem=tr_recv.at[which, d],
            device_id=at(me, z, to),
            device_id_type=MESH,
        )

    def fringe(d):
        peer = (me + d) % nc
        return pltpu.make_async_remote_copy(
            src_ref=packed.at[:, pl.ds(pl.multiple_of(peer * 128, 128), 128)],
            dst_ref=got.at[me],
            send_sem=fx_send.at[d],
            recv_sem=fx_recv.at[d],
            device_id=at(peer, z, y),
            device_id_type=MESH,
        )

    has_low, has_high = z > 0, z < nz - 1
    up = y >= NY - 2
    beyond, beyond_at = jnp.where(up, high, low), (y + 6) % 8
    reaches = (up & has_high) | (jnp.logical_not(up) & has_low)

    def share(what, n):
        ref, send, recv = ((places, pl_send, pl_recv), (packets, pk_send, pk_recv))[what]
        slot = 2 + y if n < NY else beyond_at
        return pltpu.make_async_remote_copy(
            src_ref=ref.at[2 + y],
            dst_ref=ref.at[slot],
            send_sem=send.at[n],
            recv_sem=recv.at[slot],
            device_id=at(me, z, (y + n) % NY) if n < NY else at(me, beyond, n - NY),
            device_id_type=MESH,
        )

    def share_start(what):
        for n in range(1, NY):
            share(what, n).start()

        @pl.when(reaches)
        def _():
            for n in range(NY, 2 * NY):
                share(what, n).start()

    def share_sent(what):
        for n in range(1, NY):
            share(what, n).wait_send()

        @pl.when(reaches)
        def _():
            for n in range(NY, 2 * NY):
                share(what, n).wait_send()

    def share_came(what, slot):
        ref, send, recv = ((places, pl_send, pl_recv), (packets, pk_send, pk_recv))[what]
        pltpu.make_async_remote_copy(
            src_ref=ref.at[slot],
            dst_ref=ref.at[slot],
            send_sem=send.at[0],
            recv_sem=recv.at[slot],
            device_id=at(me, z, (y + 1) % NY),
            device_id_type=MESH,
        ).wait_recv()

    for v in range(NV):
        full[v, :PAD] = jnp.zeros((PAD, ni), F32)
        full[v, PAD + nj :] = jnp.zeros((PAD, ni), F32)
        full[v, PAD : PAD + nj] = state[v]
        for d in range(1, NY):
            quarter_copy(v, d).start()
    places[2 + y] = cells[...]
    share_start(0)
    for v in range(NV):
        slab[2 + y, v] = full[v, pl.ds(pl.multiple_of(y * quarter, 8), tall), :]
    mine = pl.ds(pl.multiple_of(y * quarter, 8), quarter)
    local[0, y] = step_size[mine, :]
    local[1, y] = radius[mine, :]

    h2 = jnp.full((8, 128), coeff[0, 2], F32)
    base = (z * NY - 2).astype(F32)
    k_near = inverse_entries(
        h2,
        nz * NY,
        jnp.maximum(iota((8, 128), 0).astype(F32) + base, 0.0),
        jnp.maximum(iota((8, 128), 1).astype(F32) + base, 0.0),
    )

    def entry(a, b):
        return k_near[a : a + 1, b : b + 1]

    for q in range(4):
        for l in range(4):
            coef[q * 4 + l] = entry(2 + q, 2 + l)[0, 0]
    for side, first in ((0, 0), (1, 6)):
        a, b, d = entry(first, first), entry(first, first + 1), entry(first + 1, first + 1)
        det = 1.0 / (a * d - b * b)
        edge = (z == 0) if side == 0 else (z == nz - 1)
        for q in range(4):
            s, t = entry(2 + q, first), entry(2 + q, first + 1)
            coef[16 + side * 8 + q * 2] = jnp.where(edge, 0.0, ((s * d - t * b) * det)[0, 0])
            coef[16 + side * 8 + q * 2 + 1] = jnp.where(edge, 0.0, ((t * a - s * b) * det)[0, 0])

    for ref, length, which in ((inv_j, nj, 1), (inv_i, ni, 0)):
        ref[0], ref[1] = parts(
            inverse_entries(
                jnp.full((1, 1), coeff[0, which], F32),
                length,
                iota((length, 1), 0).astype(F32),
                iota((1, length), 1).astype(F32),
            )
        )

    turn = iter(range(-1, NV))

    def halos(v):
        for d in range(1, NY):
            quarter_copy(v, d).wait_recv()

        @pl.when(has_high)
        def _():
            halo_copy(v, 0).start()

        @pl.when(has_low)
        def _():
            halo_copy(v, 1).start()

    def between():
        v = next(turn)
        if v >= 0:
            halos(v)

    donors(state, d_cells, d_weights, d_group, packed, left, acc, between)
    for d in range(1, nc):
        fringe(d).start()
    got[me] = packed[:, pl.ds(pl.multiple_of(me * 128, 128), 128)]
    for v in turn:
        halos(v)

    for d in range(1, nc):
        fringe(d).wait_recv()
    packets[2 + y] = jnp.concatenate([got[g] for g in range(nc)], axis=1)
    share_start(1)
    for which in range(2):
        for d in range(1, NY):
            local_copy(which, d).start()

    dims = (((1,), (1,)), ((), ()))

    def place(n, carry):
        l = (n + 2) % 8
        here = ((l >= 2) | has_low) & ((l < 6) | has_high)

        @pl.when(here & (l != 2 + y))
        def _():
            share_came(0, l)
            share_came(1, l)

        for side, first in ((0, 0), (1, 6)):

            @pl.when(here & (l == first))
            def _():
                for v in range(NV):
                    halo_copy(v, side).wait_recv()

        @pl.when(jnp.logical_not(here))
        def _():
            fringed[l] = jnp.zeros((NV, tall, ni), F32)

        @pl.when(here)
        def _():
            where, values = places[l], packets[l]
            cell = jnp.concatenate([where[g : g + 1, :] for g in range(nc)], axis=1)
            row = cell // ni - (y * quarter - PAD)
            hot_i = jnp.where(iota((ni, slots), 0) == cell % ni, 1.0, 0.0).astype(BF16)
            hot_j = jnp.where(iota((tall, slots), 0) == row, 1.0, 0.0).astype(BF16)
            split = [part.astype(F32) for part in parts(values)]

            def rows_of(line):
                sixteen = jnp.broadcast_to(line, (16, slots)).astype(BF16)
                return hot_j * jnp.concatenate([sixteen] * (tall // 16), axis=0)

            for v in range(NV):
                for k in range(2):
                    lhs[(2 * v + k) * tall : (2 * v + k + 1) * tall, :] = rows_of(split[k][v : v + 1])
            lhs[2 * NV * tall :, :] = rows_of(values[NV : NV + 1])
            put = lax.dot_general(lhs[...], hot_i, dims, preferred_element_type=F32)
            filled = put[2 * NV * tall :] > 0.5
            for v in range(NV):
                hi, lo = (put[(2 * v + k) * tall : (2 * v + k + 1) * tall] for k in range(2))
                fringed[l, v] = jnp.where(filled, hi + lo, slab[l, v])

        return carry

    lax.fori_loop(0, 8, place, 0)
    for which in range(2):
        for d in range(1, NY):
            local_copy(which, d).wait_recv()

    def pass_on(t, side):
        return pltpu.make_async_remote_copy(
            src_ref=(lout, rout)[side].at[t],
            dst_ref=(lin, rin)[side].at[t],
            send_sem=sc_send.at[side, t],
            recv_sem=sc_recv.at[side, t],
            device_id=at(me, (high, low)[side], y),
            device_id_type=MESH,
        )

    @pl.when(z == 0)
    def _():
        lin[...] = jnp.zeros_like(lin)

    @pl.when(z == nz - 1)
    def _():
        rin[...] = jnp.zeros_like(rin)

    lane = iota((ROWS, ni), 1)
    for rb in range(blocks):
        top = PAD + rb * ROWS

        def layer(l, carry):
            def load(dl, dj):
                return [fringed[2 + l + dl, v, top + dj : top + dj + ROWS, :] for v in range(NV)]

            here = load(0, 0)

            def shifted(by):
                keep = (lane + by >= 0) & (lane + by < ni)
                return [jnp.where(keep, pltpu.roll(f, (-by) % ni, 1), 0.0) for f in here]

            convect, near, far = None, None, None
            for direction, look in (
                (1, shifted),
                (2, lambda by: load(0, by)),
                (3, lambda by: load(by, 0)),
            ):
                ahead, behind = look(1), look(-1)
                diff = [a - b for a, b in zip(flux(ahead, direction), flux(behind, direction))]
                one = [a + b for a, b in zip(ahead, behind)]
                two = [a + b for a, b in zip(look(2), look(-2))]
                convect = diff if convect is None else [a + b for a, b in zip(convect, diff)]
                near = one if near is None else [a + b for a, b in zip(near, one)]
                far = two if far is None else [a + b for a, b in zip(far, two)]
            dt = local[0, l, rb * ROWS : (rb + 1) * ROWS, :]
            spread = 0.0625 * local[1, l, rb * ROWS : (rb + 1) * ROWS, :]
            rhs = []
            for v in range(NV):
                smooth = far[v] - 4.0 * near[v] + 18.0 * here[v]
                rhs.append(dt * (-0.5 * convect[v] - spread * smooth))
            for v in range(NV):
                done[l, rb * NV + v] = rhs[v]
            return carry

        lax.fori_loop(0, NY, layer, 0)

        run = slice(rb * NV, (rb + 1) * NV)
        solved = product(parts(done[:, run].reshape(NY * NV * ROWS, ni)), inv_i)
        solved = solved.reshape(NY, NV, ROWS, ni)
        for v in range(NV):
            for q in range(NY):
                own[q, rb * NV + v] = (
                    coef[q * 4] * solved[0, v]
                    + coef[q * 4 + 1] * solved[1, v]
                    + coef[q * 4 + 2] * solved[2, v]
                    + coef[q * 4 + 3] * solved[3, v]
                )

        @pl.when(z == 0)
        def _():
            for t in range(rb * NV, (rb + 1) * NV):
                lout[t] = own[2:4, t]
                pass_on(t, 0).start()

        @pl.when(z == nz - 1)
        def _():
            for t in range(rb * NV, (rb + 1) * NV):
                rout[t] = own[0:2, t]
                pass_on(t, 1).start()

    def home(rb, q, source):
        run = pl.ds(rb * NV, NV)
        return pltpu.make_async_remote_copy(
            src_ref=done.at[q, run],
            dst_ref=back.at[source, run],
            send_sem=yb_send.at[rb, q],
            recv_sem=yb_recv.at[rb, source],
            device_id=at(me, z, q),
            device_id_type=MESH,
        )

    def scan_step(t, side):
        edge, other = (z == 0, z == nz - 1) if side == 0 else (z == nz - 1, z == 0)
        came, gone = ((lin, lout), (rin, rout))[side]

        @pl.when(jnp.logical_not(edge))
        def _():
            pass_on(t, side).wait_recv()

            @pl.when(jnp.logical_not(other))
            def _():
                first, second = came[t, 0], came[t, 1]
                for m in range(2):
                    q = 2 + m if side == 0 else m
                    at_q = 16 + side * 8 + q * 2
                    gone[t, m] = own[q, t] + coef[at_q] * first + coef[at_q + 1] * second
                pass_on(t, side).start()

    def finish(rb):
        for t in range(rb * NV, (rb + 1) * NV):
            l0, l1, r0, r1 = lin[t, 0], lin[t, 1], rin[t, 0], rin[t, 1]
            for q in range(NY):
                done[q, t] = (
                    own[q, t]
                    + (coef[16 + q * 2] * l0 + coef[17 + q * 2] * l1)
                    + (coef[24 + q * 2] * r0 + coef[25 + q * 2] * r1)
                )
        for q in range(NY):

            @pl.when(y == q)
            def _():
                back[q, rb * NV : (rb + 1) * NV] = done[q, rb * NV : (rb + 1) * NV]

            @pl.when(y != q)
            def _():
                home(rb, q, y).start()

    def run_scan(side, lag):
        for s in range(lag + chunks):
            if s < chunks:
                scan_step(s, side)
            if s >= lag:
                scan_step(s - lag, 1 - side)
                if (s - lag + 1) % NV == 0:
                    finish((s - lag) // NV)

    middle = nz // 2
    near = min(LAG, chunks)
    for here, side, lag in (
        (z < middle - 1, 0, chunks),
        (z == middle - 1, 0, near),
        (z == middle, 1, near),
        (z > middle, 1, chunks),
    ):

        @pl.when(here)
        def _():
            run_scan(side, lag)

    for rb in range(blocks):
        for s in range(NY):

            @pl.when(y != s)
            def _():
                home(rb, s, s).wait_recv()

    def solve(v, carry):
        plane = jnp.concatenate(
            [back[s, rb * NV + v] for s in range(NY) for rb in range(blocks)], axis=0
        )
        out[v] = product(inv_j, parts(plane))
        return carry

    lax.fori_loop(0, NV, solve, 0)

    share_sent(0)
    share_sent(1)
    for d in range(1, nc):
        fringe(d).wait_send()
    for d in range(1, NY):
        for which in range(2):
            local_copy(which, d).wait_send()
        for v in range(NV):
            quarter_copy(v, d).wait_send()
    for v in range(NV):

        @pl.when(z < nz - 1)
        def _():
            halo_copy(v, 0).wait_send()

        @pl.when(z > 0)
        def _():
            halo_copy(v, 1).wait_send()

    def drain(t, carry):
        @pl.when(z < nz - 1)
        def _():
            pass_on(t, 0).wait_send()

        @pl.when(z > 0)
        def _():
            pass_on(t, 1).wait_send()

        return carry

    lax.fori_loop(0, chunks, drain, 0)
    for rb in range(blocks):
        for q in range(NY):

            @pl.when(y != q)
            def _():
                home(rb, q, y).wait_send()


def vmem():
    return pl.BlockSpec(memory_space=pltpu.VMEM)


def body(nc, nz, state, time_step, radius, coeff, donor_cells, donor_weights, donor_group, recv_cells):
    _, nv, _, nj, ni = state.shape
    slots = recv_cells.shape[2] * recv_cells.shape[3]
    don = donor_cells.shape[3]
    quarter = nj // NY
    chunks = quarter // ROWS * NV
    field = state.reshape(nv, nj, ni)
    dma = pltpu.SemaphoreType.DMA
    delta = pl.pallas_call(
        functools.partial(step_kernel, nc, nz),
        out_shape=jax.ShapeDtypeStruct((nv, nj, ni), F32),
        in_specs=[vmem()] * 3 + [pl.BlockSpec(memory_space=pltpu.SMEM)] + [vmem()] * 4,
        out_specs=vmem(),
        scratch_shapes=[
            pltpu.VMEM((8, slots), F32),
            pltpu.VMEM((nv * nj, 2 * ni), BF16),
            pltpu.VMEM((nv, 8, don), F32),
            pltpu.VMEM((nc, 8, 128), F32),
            pltpu.VMEM((2 * NY, 8, slots), F32),
            pltpu.VMEM((2 * NY,) + recv_cells.shape[2:], jnp.int32),
            pltpu.VMEM((nv, nj + 2 * PAD, ni), F32),
            pltpu.VMEM((2 * NY, nv, quarter + 2 * PAD, ni), F32),
            pltpu.VMEM((2 * NY, nv, quarter + 2 * PAD, ni), F32),
            pltpu.VMEM((2, NY, quarter, ni), F32),
            pltpu.VMEM((NY, chunks, ROWS, ni), F32),
            pltpu.VMEM((chunks, 2, ROWS, ni), F32),
            pltpu.VMEM((chunks, 2, ROWS, ni), F32),
            pltpu.VMEM((chunks, 2, ROWS, ni), F32),
            pltpu.VMEM((chunks, 2, ROWS, ni), F32),
            pltpu.VMEM((NY, chunks, ROWS, ni), F32),
            pltpu.VMEM((NY, chunks, ROWS, ni), F32),
            pltpu.VMEM((2, nj, nj), BF16),
            pltpu.VMEM((2, ni, ni), BF16),
            pltpu.VMEM(((2 * nv + 1) * (quarter + 2 * PAD), slots), BF16),
            pltpu.SMEM((32,), F32),
            dma((nc,)), dma((nc,)),
            dma((2 * NY,)), dma((2 * NY,)),
            dma((2 * NY,)), dma((2 * NY,)),
            dma((2, NY)), dma((2, NY)),
            dma((nv, NY)), dma((nv, NY)),
            dma((nv, 2)), dma((nv, 2)),
            dma((2, chunks)), dma((2, chunks)),
            dma((quarter // ROWS, NY)), dma((quarter // ROWS, NY)),
        ],
        compiler_params=pltpu.CompilerParams(
            collective_id=0, has_side_effects=True, vmem_limit_bytes=48 * 2**20
        ),
        name="step",
    )(
        field,
        time_step.reshape(nj, ni),
        radius.reshape(nj, ni),
        coeff,
        donor_cells.reshape(donor_cells.shape[2:]),
        donor_weights.reshape(donor_weights.shape[2:]),
        donor_group.reshape(1, don),
        recv_cells.reshape(recv_cells.shape[2:]),
    )
    return delta.reshape(state.shape)


def solution(mesh):
    slabs = P("comp", "panel", None, None)
    whole = P("comp", None, "panel", None, None)
    return jax.shard_map(
        functools.partial(body, mesh.shape["comp"], mesh.shape["panel"] // NY),
        mesh=mesh,
        in_specs=(whole, slabs, slabs, P("comp", None), slabs, slabs, slabs, slabs),
        out_specs=whole,
        check_vma=False,
    )
```

```python
import functools

import jax
import jax.numpy as jnp
from jax import lax
from jax.experimental import pallas as pl
from jax.experimental.pallas import tpu as pltpu
from jax.sharding import PartitionSpec as P

MESH = pl.DeviceIdType.MESH
F32, BF16 = jnp.float32, jnp.bfloat16
NV = 5
NY = 4
PAD = 8
LAG = 12
ROWS = 8


def parts(x):
    hi = x.astype(BF16)
    return hi, (x - hi.astype(F32)).astype(BF16)


def product(a, b):
    return (
        jnp.dot(a[0], b[0], preferred_element_type=F32)
        + jnp.dot(a[0], b[1], preferred_element_type=F32)
        + jnp.dot(a[1], b[0], preferred_element_type=F32)
    )


def inverse_entries(h, length, i, j):
    root = jnp.sqrt(16.0 - 8.0 / h)
    m1, m2 = (8.0 / h) / (4.0 + root), 4.0 + root
    n = float(length)

    def green(m, a, b):
        s = 0.5 * jnp.sqrt(m)
        t = 2.0 * jnp.log(s + jnp.sqrt(1.0 + s * s))
        d = jnp.abs(a - b)
        top = (
            jnp.exp(-t * d)
            - jnp.exp(-t * (a + b + 2.0))
            - jnp.exp(-t * (2.0 * n - a - b))
            + jnp.exp(-t * (2.0 * n + 2.0 - d))
        )
        two_sinh = jnp.exp(t) - jnp.exp(-t)
        return top / (two_sinh * (1.0 - jnp.exp(-2.0 * t * (n + 1.0))))

    def smooth(a, b):
        return (8.0 / h) * (green(m1, a, b) - green(m2, a, b)) / (m2 - m1)

    zero = jnp.zeros_like(h)
    corner, across = smooth(zero, zero), smooth(zero, zero + (n - 1.0))
    even_scale = 0.5 / (8.0 / h + corner + across)
    odd_scale = 0.5 / (8.0 / h + corner - across)
    i0, i1 = smooth(i, zero), smooth(i, zero + (n - 1.0))
    j0, j1 = smooth(j, zero), smooth(j, zero + (n - 1.0))
    return (
        smooth(i, j)
        - even_scale * (i0 + i1) * (j0 + j1)
        - odd_scale * (i0 - i1) * (j0 - j1)
    )


def iota(shape, axis):
    return lax.broadcasted_iota(jnp.int32, shape, axis)


def donors(state, cells, weights, group, packed, left, acc, between):
    nv, nj, ni = state.shape
    n_c, don = cells.shape
    count = packed.shape[1] // 128
    width = min(256, don)
    flat = state[...].reshape(nv * nj, ni)
    for k, part in enumerate(parts(flat)):
        left[:, k * ni : (k + 1) * ni] = part
    acc[...] = jnp.zeros_like(acc)

    for block in range(don // width):
        span = slice(block * width, (block + 1) * width)

        def one(c, carry):
            cell = cells[pl.ds(c, 1), span]
            weight = weights[pl.ds(c, 1), span]
            col = jnp.where(iota((ni, width), 0) == cell % ni, 1.0, 0.0).astype(BF16)
            got = jnp.dot(
                left[...], jnp.concatenate([col, col], axis=0), preferred_element_type=F32
            )
            row = jnp.where(iota((nj, width), 0) == cell // ni, weight, 0.0)
            for v in range(nv):
                term = got[v * nj : (v + 1) * nj] * row
                acc[v, :, span] += jnp.sum(term.reshape(nj // 8, 8, width), axis=0)
            return carry

        for half in range(2):
            lax.fori_loop(half * n_c // 2, (half + 1) * n_c // 2, one, 0)
            between()

    values = [jnp.sum(acc[v], axis=0, keepdims=True) for v in range(nv)]
    values = jnp.concatenate(
        values + [jnp.ones((1, don), F32), jnp.zeros((8 - nv - 1, don), F32)], axis=0
    )
    mine = group[...]
    hot = jnp.where(iota((16, don), 0) == mine, 1.0, 0.0)
    before = jnp.where(iota((don, don), 0) < iota((don, don), 1), 1.0, 0.0).astype(BF16)
    ahead = jnp.dot(hot.astype(BF16), before, preferred_element_type=F32)
    target = mine * 128 + jnp.sum(hot * ahead, axis=0, keepdims=True).astype(jnp.int32)
    place = jnp.where(iota((count * 128, don), 0) == target, 1.0, 0.0).astype(BF16)
    dims = (((1,), (1,)), ((), ()))
    hi, lo = parts(values)
    packed[...] = lax.dot_general(hi, place, dims, preferred_element_type=F32) + lax.dot_general(
        lo, place, dims, preferred_element_type=F32
    )


def flux(f, direction):
    rho = jnp.where(f[0] > 0.0, f[0], 1.0)
    inv = 1.0 / rho
    speed = f[direction] * inv
    pressure = 0.4 * (f[4] - 0.5 * (f[1] * f[1] + f[2] * f[2] + f[3] * f[3]) * inv)
    out = [f[direction]]
    for member in (1, 2, 3):
        term = f[member] * speed
        out.append(term + pressure if member == direction else term)
    out.append((f[4] + pressure) * speed)
    return out


def step_kernel(
    nc, nz, state, step_size, radius, coeff, d_cells, d_weights, d_group, cells, out,
    packed, left, acc, got, packets, places, full, slab, fringed, local, own, lin, lout, rin, rout, done, back, inv_j, inv_i, lhs, coef,
    fx_send, fx_recv, pk_send, pk_recv, pl_send, pl_recv, tr_send, tr_recv, ya_send, ya_recv, zh_send, zh_recv, sc_send, sc_recv, yb_send, yb_recv,
):
    _, nj, ni = state.shape
    quarter = nj // NY
    tall = quarter + 2 * PAD
    blocks = quarter // ROWS
    chunks = blocks * NV
    slots = packed.shape[1]
    me = lax.axis_index("comp")
    panel = lax.axis_index("panel")
    z, y = panel // NY, panel % NY
    low, high = (z + nz - 1) % nz, (z + 1) % nz

    def at(comp, z_, y_):
        return (comp, z_ * NY + y_)

    barrier = pltpu.get_barrier_semaphore()
    for d in range(1, nc):
        pl.semaphore_signal(barrier, inc=1, device_id=at((me + d) % nc, z, y), device_id_type=MESH)
    for d in range(1, NY):
        pl.semaphore_signal(barrier, inc=1, device_id=at(me, z, (y + d) % NY), device_id_type=MESH)
    for q in range(NY):
        pl.semaphore_signal(barrier, inc=1, device_id=at(me, low, q), device_id_type=MESH)
        pl.semaphore_signal(barrier, inc=1, device_id=at(me, high, q), device_id_type=MESH)
    pl.semaphore_wait(barrier, nc - 1 + NY - 1 + 2 * NY)

    def quarter_copy(v, d):
        to = (y + d) % NY
        return pltpu.make_async_remote_copy(
            src_ref=full.at[v, pl.ds(pl.multiple_of(to * quarter, 8), tall), :],
            dst_ref=slab.at[2 + y, v],
            send_sem=ya_send.at[v, d],
            recv_sem=ya_recv.at[v, d],
            device_id=at(me, z, to),
            device_id_type=MESH,
        )

    def halo_copy(v, side):
        return pltpu.make_async_remote_copy(
            src_ref=slab.at[pl.ds(4 - 2 * side, 2), v, pl.ds(PAD, quarter), :],
            dst_ref=slab.at[pl.ds(6 * side, 2), v, pl.ds(PAD, quarter), :],
            send_sem=zh_send.at[v, side],
            recv_sem=zh_recv.at[v, side],
            device_id=at(me, (high, low)[side], y),
            device_id_type=MESH,
        )

    def local_copy(which, d):
        to = (y + d) % NY
        return pltpu.make_async_remote_copy(
            src_ref=(step_size, radius)[which].at[pl.ds(pl.multiple_of(to * quarter, 8), quarter), :],
            dst_ref=local.at[which, y],
            send_sem=tr_send.at[which, d],
            recv_sem=tr_recv.at[which, d],
            device_id=at(me, z, to),
            device_id_type=MESH,
        )

    def fringe(d):
        peer = (me + d) % nc
        return pltpu.make_async_remote_copy(
            src_ref=packed.at[:, pl.ds(pl.multiple_of(peer * 128, 128), 128)],
            dst_ref=got.at[me],
            send_sem=fx_send.at[d],
            recv_sem=fx_recv.at[d],
            device_id=at(peer, z, y),
            device_id_type=MESH,
        )

    has_low, has_high = z > 0, z < nz - 1
    up = y >= NY - 2
    beyond, beyond_at = jnp.where(up, high, low), (y + 6) % 8
    reaches = (up & has_high) | (jnp.logical_not(up) & has_low)

    def share(what, n):
        ref, send, recv = ((places, pl_send, pl_recv), (packets, pk_send, pk_recv))[what]
        slot = 2 + y if n < NY else beyond_at
        return pltpu.make_async_remote_copy(
            src_ref=ref.at[2 + y],
            dst_ref=ref.at[slot],
            send_sem=send.at[n],
            recv_sem=recv.at[slot],
            device_id=at(me, z, (y + n) % NY) if n < NY else at(me, beyond, n - NY),
            device_id_type=MESH,
        )

    def share_start(what):
        for n in range(1, NY):
            share(what, n).start()

        @pl.when(reaches)
        def _():
            for n in range(NY, 2 * NY):
                share(what, n).start()

    def share_sent(what):
        for n in range(1, NY):
            share(what, n).wait_send()

        @pl.when(reaches)
        def _():
            for n in range(NY, 2 * NY):
                share(what, n).wait_send()

    def share_came(what, slot):
        ref, send, recv = ((places, pl_send, pl_recv), (packets, pk_send, pk_recv))[what]
        pltpu.make_async_remote_copy(
            src_ref=ref.at[slot],
            dst_ref=ref.at[slot],
            send_sem=send.at[0],
            recv_sem=recv.at[slot],
            device_id=at(me, z, (y + 1) % NY),
            device_id_type=MESH,
        ).wait_recv()

    for v in range(NV):
        full[v, :PAD] = jnp.zeros((PAD, ni), F32)
        full[v, PAD + nj :] = jnp.zeros((PAD, ni), F32)
        full[v, PAD : PAD + nj] = state[v]
        for d in range(1, NY):
            quarter_copy(v, d).start()
    places[2 + y] = cells[...]
    share_start(0)
    for v in range(NV):
        slab[2 + y, v] = full[v, pl.ds(pl.multiple_of(y * quarter, 8), tall), :]
    mine = pl.ds(pl.multiple_of(y * quarter, 8), quarter)
    local[0, y] = step_size[mine, :]
    local[1, y] = radius[mine, :]

    h2 = jnp.full((8, 128), coeff[0, 2], F32)
    base = (z * NY - 2).astype(F32)
    k_near = inverse_entries(
        h2,
        nz * NY,
        jnp.maximum(iota((8, 128), 0).astype(F32) + base, 0.0),
        jnp.maximum(iota((8, 128), 1).astype(F32) + base, 0.0),
    )

    def entry(a, b):
        return k_near[a : a + 1, b : b + 1]

    for q in range(4):
        for l in range(4):
            coef[q * 4 + l] = entry(2 + q, 2 + l)[0, 0]
    for side, first in ((0, 0), (1, 6)):
        a, b, d = entry(first, first), entry(first, first + 1), entry(first + 1, first + 1)
        det = 1.0 / (a * d - b * b)
        edge = (z == 0) if side == 0 else (z == nz - 1)
        for q in range(4):
            s, t = entry(2 + q, first), entry(2 + q, first + 1)
            coef[16 + side * 8 + q * 2] = jnp.where(edge, 0.0, ((s * d - t * b) * det)[0, 0])
            coef[16 + side * 8 + q * 2 + 1] = jnp.where(edge, 0.0, ((t * a - s * b) * det)[0, 0])

    for ref, length, which in ((inv_j, nj, 1), (inv_i, ni, 0)):
        ref[0], ref[1] = parts(
            inverse_entries(
                jnp.full((1, 1), coeff[0, which], F32),
                length,
                iota((length, 1), 0).astype(F32),
                iota((1, length), 1).astype(F32),
            )
        )

    turn = iter(range(-1, NV))

    def halos(v):
        for d in range(1, NY):
            quarter_copy(v, d).wait_recv()

        @pl.when(has_high)
        def _():
            halo_copy(v, 0).start()

        @pl.when(has_low)
        def _():
            halo_copy(v, 1).start()

    def between():
        v = next(turn)
        if v >= 0:
            halos(v)

    donors(state, d_cells, d_weights, d_group, packed, left, acc, between)
    for d in range(1, nc):
        fringe(d).start()
    got[me] = packed[:, pl.ds(pl.multiple_of(me * 128, 128), 128)]
    for v in turn:
        halos(v)

    for d in range(1, nc):
        fringe(d).wait_recv()
    packets[2 + y] = jnp.concatenate([got[g] for g in range(nc)], axis=1)
    share_start(1)
    for which in range(2):
        for d in range(1, NY):
            local_copy(which, d).start()

    dims = (((1,), (1,)), ((), ()))

    def place(n, carry):
        l = (n + 2) % 8
        here = ((l >= 2) | has_low) & ((l < 6) | has_high)

        @pl.when(here & (l != 2 + y))
        def _():
            share_came(0, l)
            share_came(1, l)

        for side, first in ((0, 0), (1, 6)):

            @pl.when(here & (l == first))
            def _():
                for v in range(NV):
                    halo_copy(v, side).wait_recv()

        @pl.when(jnp.logical_not(here))
        def _():
            fringed[l] = jnp.zeros((NV, tall, ni), F32)

        @pl.when(here)
        def _():
            where, values = places[l], packets[l]
            cell = jnp.concatenate([where[g : g + 1, :] for g in range(nc)], axis=1)
            row = cell // ni - (y * quarter - PAD)
            hot_i = jnp.where(iota((ni, slots), 0) == cell % ni, 1.0, 0.0).astype(BF16)
            hot_j = jnp.where(iota((tall, slots), 0) == row, 1.0, 0.0).astype(BF16)
            split = [part.astype(F32) for part in parts(values)]

            def rows_of(line):
                sixteen = jnp.broadcast_to(line, (16, slots)).astype(BF16)
                return hot_j * jnp.concatenate([sixteen] * (tall // 16), axis=0)

            for v in range(NV):
                for k in range(2):
                    lhs[(2 * v + k) * tall : (2 * v + k + 1) * tall, :] = rows_of(split[k][v : v + 1])
            lhs[2 * NV * tall :, :] = rows_of(values[NV : NV + 1])
            put = lax.dot_general(lhs[...], hot_i, dims, preferred_element_type=F32)
            filled = put[2 * NV * tall :] > 0.5
            for v in range(NV):
                hi, lo = (put[(2 * v + k) * tall : (2 * v + k + 1) * tall] for k in range(2))
                fringed[l, v] = jnp.where(filled, hi + lo, slab[l, v])

        return carry

    lax.fori_loop(0, 8, place, 0)
    for which in range(2):
        for d in range(1, NY):
            local_copy(which, d).wait_recv()

    def pass_on(t, side):
        return pltpu.make_async_remote_copy(
            src_ref=(lout, rout)[side].at[t],
            dst_ref=(lin, rin)[side].at[t],
            send_sem=sc_send.at[side, t],
            recv_sem=sc_recv.at[side, t],
            device_id=at(me, (high, low)[side], y),
            device_id_type=MESH,
        )

    @pl.when(z == 0)
    def _():
        lin[...] = jnp.zeros_like(lin)

    @pl.when(z == nz - 1)
    def _():
        rin[...] = jnp.zeros_like(rin)

    lane = iota((ROWS, ni), 1)
    for rb in range(blocks):
        top = PAD + rb * ROWS

        def layer(l, carry):
            def load(dl, dj):
                return [fringed[2 + l + dl, v, top + dj : top + dj + ROWS, :] for v in range(NV)]

            here = load(0, 0)

            def shifted(by):
                keep = (lane + by >= 0) & (lane + by < ni)
                return [jnp.where(keep, pltpu.roll(f, (-by) % ni, 1), 0.0) for f in here]

            convect, near, far = None, None, None
            for direction, look in (
                (1, shifted),
                (2, lambda by: load(0, by)),
                (3, lambda by: load(by, 0)),
            ):
                ahead, behind = look(1), look(-1)
                diff = [a - b for a, b in zip(flux(ahead, direction), flux(behind, direction))]
                one = [a + b for a, b in zip(ahead, behind)]
                two = [a + b for a, b in zip(look(2), look(-2))]
                convect = diff if convect is None else [a + b for a, b in zip(convect, diff)]
                near = one if near is None else [a + b for a, b in zip(near, one)]
                far = two if far is None else [a + b for a, b in zip(far, two)]
            dt = local[0, l, rb * ROWS : (rb + 1) * ROWS, :]
            spread = 0.0625 * local[1, l, rb * ROWS : (rb + 1) * ROWS, :]
            rhs = []
            for v in range(NV):
                smooth = far[v] - 4.0 * near[v] + 18.0 * here[v]
                rhs.append(dt * (-0.5 * convect[v] - spread * smooth))
            for v in range(NV):
                done[l, rb * NV + v] = rhs[v]
            return carry

        lax.fori_loop(0, NY, layer, 0)

        run = slice(rb * NV, (rb + 1) * NV)
        solved = product(parts(done[:, run].reshape(NY * NV * ROWS, ni)), inv_i)
        solved = solved.reshape(NY, NV, ROWS, ni)
        for v in range(NV):
            for q in range(NY):
                own[q, rb * NV + v] = (
                    coef[q * 4] * solved[0, v]
                    + coef[q * 4 + 1] * solved[1, v]
                    + coef[q * 4 + 2] * solved[2, v]
                    + coef[q * 4 + 3] * solved[3, v]
                )

        @pl.when(z == 0)
        def _():
            for t in range(rb * NV, (rb + 1) * NV):
                lout[t] = own[2:4, t]
                pass_on(t, 0).start()

        @pl.when(z == nz - 1)
        def _():
            for t in range(rb * NV, (rb + 1) * NV):
                rout[t] = own[0:2, t]
                pass_on(t, 1).start()

    def home(rb, q, source):
        run = pl.ds(rb * NV, NV)
        return pltpu.make_async_remote_copy(
            src_ref=done.at[q, run],
            dst_ref=back.at[source, run],
            send_sem=yb_send.at[rb, q],
            recv_sem=yb_recv.at[rb, source],
            device_id=at(me, z, q),
            device_id_type=MESH,
        )

    def scan_step(t, side):
        edge, other = (z == 0, z == nz - 1) if side == 0 else (z == nz - 1, z == 0)
        came, gone = ((lin, lout), (rin, rout))[side]

        @pl.when(jnp.logical_not(edge))
        def _():
            pass_on(t, side).wait_recv()

            @pl.when(jnp.logical_not(other))
            def _():
                first, second = came[t, 0], came[t, 1]
                for m in range(2):
                    q = 2 + m if side == 0 else m
                    at_q = 16 + side * 8 + q * 2
                    gone[t, m] = own[q, t] + coef[at_q] * first + coef[at_q + 1] * second
                pass_on(t, side).start()

    def finish(rb):
        for t in range(rb * NV, (rb + 1) * NV):
            l0, l1, r0, r1 = lin[t, 0], lin[t, 1], rin[t, 0], rin[t, 1]
            for q in range(NY):
                done[q, t] = (
                    own[q, t]
                    + (coef[16 + q * 2] * l0 + coef[17 + q * 2] * l1)
                    + (coef[24 + q * 2] * r0 + coef[25 + q * 2] * r1)
                )
        for q in range(NY):

            @pl.when(y == q)
            def _():
                back[q, rb * NV : (rb + 1) * NV] = done[q, rb * NV : (rb + 1) * NV]

            @pl.when(y != q)
            def _():
                home(rb, q, y).start()

    def run_scan(side, lag):
        for s in range(lag + chunks):
            if s < chunks:
                scan_step(s, side)
            if s >= lag:
                scan_step(s - lag, 1 - side)
                if (s - lag + 1) % NV == 0:
                    finish((s - lag) // NV)

    middle = nz // 2
    near = min(LAG, chunks)
    for here, side, lag in (
        (z < middle - 1, 0, chunks),
        (z == middle - 1, 0, near),
        (z == middle, 1, near),
        (z > middle, 1, chunks),
    ):

        @pl.when(here)
        def _():
            run_scan(side, lag)

    for rb in range(blocks):
        for s in range(NY):

            @pl.when(y != s)
            def _():
                home(rb, s, s).wait_recv()

    def solve(v, carry):
        plane = jnp.concatenate(
            [back[s, rb * NV + v] for s in range(NY) for rb in range(blocks)], axis=0
        )
        out[v] = product(inv_j, parts(plane))
        return carry

    lax.fori_loop(0, NV, solve, 0)

    share_sent(0)
    share_sent(1)
    for d in range(1, nc):
        fringe(d).wait_send()
    for d in range(1, NY):
        for which in range(2):
            local_copy(which, d).wait_send()
        for v in range(NV):
            quarter_copy(v, d).wait_send()
    for v in range(NV):

        @pl.when(z < nz - 1)
        def _():
            halo_copy(v, 0).wait_send()

        @pl.when(z > 0)
        def _():
            halo_copy(v, 1).wait_send()

    def drain(t, carry):
        @pl.when(z < nz - 1)
        def _():
            pass_on(t, 0).wait_send()

        @pl.when(z > 0)
        def _():
            pass_on(t, 1).wait_send()

        return carry

    lax.fori_loop(0, chunks, drain, 0)
    for rb in range(blocks):
        for q in range(NY):

            @pl.when(y != q)
            def _():
                home(rb, q, y).wait_send()


def vmem():
    return pl.BlockSpec(memory_space=pltpu.VMEM)


def body(nc, nz, state, time_step, radius, coeff, donor_cells, donor_weights, donor_group, recv_cells):
    _, nv, _, nj, ni = state.shape
    slots = recv_cells.shape[2] * recv_cells.shape[3]
    don = donor_cells.shape[3]
    quarter = nj // NY
    chunks = quarter // ROWS * NV
    field = state.reshape(nv, nj, ni)
    dma = pltpu.SemaphoreType.DMA
    delta = pl.pallas_call(
        functools.partial(step_kernel, nc, nz),
        out_shape=jax.ShapeDtypeStruct((nv, nj, ni), F32),
        in_specs=[vmem()] * 3 + [pl.BlockSpec(memory_space=pltpu.SMEM)] + [vmem()] * 4,
        out_specs=vmem(),
        scratch_shapes=[
            pltpu.VMEM((8, slots), F32),
            pltpu.VMEM((nv * nj, 2 * ni), BF16),
            pltpu.VMEM((nv, 8, don), F32),
            pltpu.VMEM((nc, 8, 128), F32),
            pltpu.VMEM((2 * NY, 8, slots), F32),
            pltpu.VMEM((2 * NY,) + recv_cells.shape[2:], jnp.int32),
            pltpu.VMEM((nv, nj + 2 * PAD, ni), F32),
            pltpu.VMEM((2 * NY, nv, quarter + 2 * PAD, ni), F32),
            pltpu.VMEM((2 * NY, nv, quarter + 2 * PAD, ni), F32),
            pltpu.VMEM((2, NY, quarter, ni), F32),
            pltpu.VMEM((NY, chunks, ROWS, ni), F32),
            pltpu.VMEM((chunks, 2, ROWS, ni), F32),
            pltpu.VMEM((chunks, 2, ROWS, ni), F32),
            pltpu.VMEM((chunks, 2, ROWS, ni), F32),
            pltpu.VMEM((chunks, 2, ROWS, ni), F32),
            pltpu.VMEM((NY, chunks, ROWS, ni), F32),
            pltpu.VMEM((NY, chunks, ROWS, ni), F32),
            pltpu.VMEM((2, nj, nj), BF16),
            pltpu.VMEM((2, ni, ni), BF16),
            pltpu.VMEM(((2 * nv + 1) * (quarter + 2 * PAD), slots), BF16),
            pltpu.SMEM((32,), F32),
            dma((nc,)), dma((nc,)),
            dma((2 * NY,)), dma((2 * NY,)),
            dma((2 * NY,)), dma((2 * NY,)),
            dma((2, NY)), dma((2, NY)),
            dma((nv, NY)), dma((nv, NY)),
            dma((nv, 2)), dma((nv, 2)),
            dma((2, chunks)), dma((2, chunks)),
            dma((quarter // ROWS, NY)), dma((quarter // ROWS, NY)),
        ],
        compiler_params=pltpu.CompilerParams(
            collective_id=0, has_side_effects=True, vmem_limit_bytes=48 * 2**20
        ),
        name="step",
    )(
        field,
        time_step.reshape(nj, ni),
        radius.reshape(nj, ni),
        coeff,
        donor_cells.reshape(donor_cells.shape[2:]),
        donor_weights.reshape(donor_weights.shape[2:]),
        donor_group.reshape(1, don),
        recv_cells.reshape(recv_cells.shape[2:]),
    )
    return delta.reshape(state.shape)


def solution(mesh):
    slabs = P("comp", "panel", None, None)
    whole = P("comp", None, "panel", None, None)
    return jax.shard_map(
        functools.partial(body, mesh.shape["comp"], mesh.shape["panel"] // NY),
        mesh=mesh,
        in_specs=(whole, slabs, slabs, P("comp", None), slabs, slabs, slabs, slabs),
        out_specs=whole,
        check_vma=False,
    )
```
